32 devices in a mesh: chan: 4 (over z), frame: 8 (over y, x, core).
Axes of the slice: x: 2, y: 2, z: 4, core: 2. Of those that a mesh axis runs over, the one named last changes fastest.
Arguments:
- rf_data: bfloat16 [2, 8, 256, 1024], P(None, None, 'frame', 'chan'), may hold values from -6 to 6
- elem_pos: int32 [3, 1024], replicated, may hold values from -16 to 15, as said below
- vox_pos: int32 [3, 4096], P(None, 'chan'), may hold values from -32 to 62, as said below
- subbands: int32 [8], replicated, may hold values from 0 to 63, as said below
Outputs:
- filtered: bfloat16 [256, 2, 8, 4096], P('frame', None, None, 'chan')
The draws below stay inside these ranges and needn't reach their ends.
Inputs may be any that keep to these rules, and one draw needn't show every extreme that they name: `elem_pos`: the element positions are the 32 x 32 grid with x and y from -16, each point once in a drawn order; z is 0, 1 or 2. `vox_pos`: distinct voxels of a box: x and y from -32 to 31, z from 48 to 62 in steps of 2. `subbands`: 8 distinct bin numbers.
All inputs are finite; a program needn't handle non-finite values.
Results may differ from the reference program's by a relative error of at most 0.0075.
Values may be sent and summed in bfloat16 or wider, within the bound.
A program may use at most 128 MiB of HBM per device.

```python
import math
import jax
import jax.numpy as jnp
from jax import lax

SIDE = 32
C = 1024
F = 256
B = 8
V = 4096


def draw_elem_pos(key, part):
    order = jax.random.permutation(jax.random.fold_in(key, 11), SIDE * SIDE).astype(jnp.int32)
    pos_x = order % SIDE - SIDE // 2
    pos_y = order // SIDE - SIDE // 2
    pos_z = jax.random.randint(jax.random.fold_in(key, 12), (SIDE * SIDE,), 0, 3).astype(jnp.int32)
    return jnp.stack([pos_x, pos_y, pos_z], axis=0).astype(jnp.int32)


def draw_vox_pos(key, part):
    middle = (jax.random.permutation(jax.random.fold_in(key, 21), 32766)[:V - 2] + 1).astype(jnp.int32)
    ends = jnp.array([0, 32767], dtype=jnp.int32)
    joined = jnp.concatenate([ends, middle]).astype(jnp.int32)
    chosen = jax.random.permutation(jax.random.fold_in(key, 22), joined).astype(jnp.int32)
    pos_x = chosen % 64 - 32
    pos_y = chosen // 64 % 64 - 32
    pos_z = 48 + 2 * (chosen // 4096)
    return jnp.stack([pos_x, pos_y, pos_z], axis=0).astype(jnp.int32)


def draw_subbands(key, part):
    middle = (jax.random.permutation(jax.random.fold_in(key, 31), 62)[:B - 2] + 1).astype(jnp.int32)
    ends = jnp.array([0, 63], dtype=jnp.int32)
    joined = jnp.concatenate([ends, middle]).astype(jnp.int32)
    return jax.random.permutation(jax.random.fold_in(key, 32), joined).astype(jnp.int32)


def block_scale(rng, dims, pieces, low, largest):
    level = 1.0
    for position, shards_of in pieces:
        draws = jax.random.uniform(jax.random.fold_in(jax.random.fold_in(rng, 6), position), (shards_of,), jnp.float32, low / len(pieces), largest / len(pieces))
        level = level * jnp.repeat(jnp.exp(draws), dims[position] // shards_of).reshape((-1,) + (1,) * (len(dims) - 1 - position))
    return level


def scatter_about(key, dims, width, bound, split=(), held_as=jnp.bfloat16):
    entries = jax.random.normal(key, dims, jnp.float32) * width
    if len(split) > 0:
        entries = block_scale(key, dims, split, -0.22, 0.18) * entries
    return jnp.clip(entries, min=-bound, max=bound).astype(held_as)


def setup_inputs(seed: int = 0) -> dict:
    splits = jax.random.split(jax.random.key(seed), 5)
    rf_data = scatter_about(splits[0], (2, B, F, C), 1.0, 6.0, ((2, 8), (3, 4)))
    elem_pos = draw_elem_pos(jax.random.fold_in(splits[4], 71), 0)
    vox_pos = draw_vox_pos(jax.random.fold_in(splits[4], 71), 0)
    subbands = draw_subbands(jax.random.fold_in(splits[4], 71), 0)
    return dict(rf_data=rf_data, elem_pos=elem_pos, vox_pos=vox_pos, subbands=subbands)


TWO_PI = 2.0 * math.pi
EPSILON = 1e-06

def geometry(elem_pos, vox_pos):
    elem = elem_pos.astype(jnp.float32)
    voxel = vox_pos.astype(jnp.float32)
    delta_x = voxel[0][:, None] - elem[0][None, :]
    delta_y = voxel[1][:, None] - elem[1][None, :]
    delta_z = voxel[2][:, None] - elem[2][None, :]
    distance = jnp.sqrt(delta_x * delta_x + delta_y * delta_y + delta_z * delta_z)
    inverse = 1.0 / math.sqrt(elem_pos.shape[1])
    weight = delta_z / distance * inverse
    travel = voxel[2][:, None] + distance
    return (weight, travel)

def data_matrix(rf_data):
    data_re = jnp.swapaxes(rf_data[0], 1, 2)
    data_im = jnp.swapaxes(rf_data[1], 1, 2)
    upper_rows = jnp.concatenate([data_re, data_im], axis=2)
    lower_rows = jnp.concatenate([-data_im, data_re], axis=2)
    return jnp.concatenate([upper_rows, lower_rows], axis=1)

def complex_product(left_pair, right_pair):
    first_re, first_im = left_pair
    second_re, second_im = right_pair
    high = lax.Precision.HIGHEST
    real_part = jnp.einsum('bij,bjk->bik', first_re, second_re, precision=high) - jnp.einsum('bij,bjk->bik', first_im, second_im, precision=high)
    imag_part = jnp.einsum('bij,bjk->bik', first_re, second_im, precision=high) + jnp.einsum('bij,bjk->bik', first_im, second_re, precision=high)
    return (real_part, imag_part)

def filter_matrix(gram):
    gram_re = gram[:, 0]
    gram_im = gram[:, 1]
    frames = gram.shape[2]
    squares = lax.optimization_barrier(jnp.sum(gram_re * gram_re + gram_im * gram_im, axis=(1, 2)))
    factor = 4.0 / jnp.sqrt(squares + EPSILON)
    mat_re = gram_re * factor[:, None, None]
    mat_im = gram_im * factor[:, None, None]
    second = complex_product((mat_re, mat_im), (mat_re, mat_im))
    third = complex_product(second, (mat_re, mat_im))
    identity = jnp.eye(frames, dtype=jnp.float32)[None]
    filter_re = identity - mat_re + 0.3 * second[0] - 0.03 * third[0]
    filter_im = -mat_im + 0.3 * second[1] - 0.03 * third[1]
    return jnp.stack([filter_re, filter_im], axis=1).astype(jnp.bfloat16)

def block_filter(filter_bf):
    filter_re = filter_bf[:, 0]
    filter_im = filter_bf[:, 1]
    upper_rows = jnp.concatenate([filter_re, filter_im], axis=2)
    lower_rows = jnp.concatenate([-filter_im, filter_re], axis=2)
    return jnp.concatenate([upper_rows, lower_rows], axis=1)

def reference(rf_data, elem_pos, vox_pos, subbands):
    weight, travel = geometry(elem_pos, vox_pos)
    wavenum = (32.0 + subbands.astype(jnp.float32)) / 64.0
    matrix = data_matrix(rf_data)

    def one_bin(index):
        phase_angle = TWO_PI * wavenum[index] * travel
        operator = jnp.concatenate([weight * jnp.cos(phase_angle), -(weight * jnp.sin(phase_angle))], axis=1).astype(jnp.bfloat16)
        return jnp.dot(operator, matrix[index], preferred_element_type=jnp.float32).astype(jnp.bfloat16)
    volumes = lax.map(one_bin, jnp.arange(B, dtype=jnp.int32))
    stacked = jnp.swapaxes(volumes, 0, 1).astype(jnp.float32)
    products = jnp.einsum('vbi,vbj->bij', stacked, stacked, precision=lax.Precision.HIGHEST)
    gram_re = products[:, :F, :F] + products[:, F:, F:]
    gram_im = products[:, :F, F:] - products[:, F:, :F]
    gram = jnp.stack([gram_re, gram_im], axis=1)
    filter_bf = filter_matrix(gram)
    blocks = block_filter(filter_bf).astype(jnp.float32)
    applied = jnp.einsum('vbi,bij->vbj', stacked, blocks, precision=lax.Precision.HIGHEST).astype(jnp.bfloat16)
    applied = applied.reshape(applied.shape[0], B, 2, F)
    return jnp.transpose(applied, (3, 2, 1, 0))
```

```python
import functools
import math

import jax
import jax.numpy as jnp
from jax import lax
from jax.experimental import pallas as pl
from jax.experimental.pallas import tpu as pltpu
from jax.sharding import PartitionSpec as P

EPSILON = 1e-06
MESH = pl.DeviceIdType.MESH
F32 = jnp.float32
BF16 = jnp.bfloat16
SIN_POLY = (3.1415820121765137, -5.167142868041992, 2.5418989658355713, -0.5546361804008484)
COS_POLY = (0.9999933242797852, -4.933938026428223, 4.04128360748291, -1.222127079963684)
LANES = 128
ROUND = 12582912.0
TALL = 16
REACH = 2
GO_AT = 7


def horner(coefs, z):
    value = coefs[-1] * z + coefs[-2]
    for coef in coefs[-3::-1]:
        value = value * z + coef
    return value


def dot(a, b):
    return jnp.dot(a, b, preferred_element_type=F32)


def dot_nt(a, b):
    return lax.dot_general(a, b, (((1,), (1,)), ((), ())), preferred_element_type=F32)


def kernel(
    nc, nf, nbins,
    rf_ref, elem_hbm, vox_hbm, sub_hbm, out_ref,
    rfbuf, elem_ref, vox_ref, sub_ref, in_sem, elem, vox, oper, acc, vols, part, slabs, total, hmat, sent,
    go_sem, own_sem, plane_send, plane_recv, line_send, relay_send, line_recv,
    rs_send, rs_recv, ag_send, ag_recv, out_own, out_send, out_recv,
):
    share = nf // nbins
    stagger = share == 1 and nf % 2 == 0
    frames = rfbuf.shape[2]
    cl = rfbuf.shape[3]
    chans = nc * cl
    vd = vols.shape[1]
    fl = frames // nf
    halves = nf // 2
    width = vd // halves
    rows = frames // 2
    owners = ((nc // 2 - 1, 0), (nc // 2, 0))
    me_c = lax.axis_index("chan")
    me_f = lax.axis_index("frame")
    me_bin = lax.div(me_f, share)
    me_sub = lax.rem(me_f, share)
    second = lax.rem(me_f, 2) == 1
    first_core = jnp.logical_not(second)
    def partner(k):
        j = 0
        bit = 1
        while bit < nf:
            a = lax.rem(lax.div(me_f, bit), 2)
            b = k // bit % 2 if isinstance(k, int) else lax.rem(lax.div(k, bit), 2)
            j = j + bit * (a + b - 2 * a * b)
            bit *= 2
        return j

    def if_first(run, *conditions):
        for condition in conditions + ((first_core,) if stagger else ()):
            run = functools.partial(pl.when(condition), run)
        run()

    def piece(j):
        return pl.ds(pl.multiple_of(j * fl, fl), fl)

    barrier = pltpu.get_barrier_semaphore()
    for k in range(1, nf):
        pl.semaphore_signal(barrier, inc=1, device_id=(me_c, partner(k)), device_id_type=MESH)
    for k in range(1, nc):
        for s in range(share):
            other = (lax.rem(me_c + k, nc), me_bin * share + s)
            pl.semaphore_signal(barrier, inc=1, device_id=other, device_id_type=MESH)

    mine = piece(me_f)
    loads = [
        pltpu.make_async_copy(source, place, in_sem.at[index])
        for index, (source, place) in enumerate(
            ((elem_hbm, elem_ref), (vox_hbm, vox_ref), (sub_hbm, sub_ref)))
    ]
    for load in loads:
        load.start()
    own = pltpu.make_async_copy(rf_ref.at[:, me_bin], rfbuf.at[me_c, :, mine], own_sem)
    own.start()
    pl.semaphore_wait(barrier, nf - 1 + (nc - 1) * share)

    def plane_copy(j):
        return pltpu.make_async_remote_copy(
            src_ref=rf_ref.at[:, lax.div(j, share)], dst_ref=rfbuf.at[me_c, :, mine],
            send_sem=plane_send.at[j], recv_sem=plane_recv.at[me_f],
            device_id=(me_c, j), device_id_type=MESH)

    def plane_arrival(j):
        return pltpu.make_async_remote_copy(
            src_ref=rf_ref.at[:, 0], dst_ref=rfbuf.at[me_c, :, piece(j)], send_sem=plane_send.at[j],
            recv_sem=plane_recv.at[j], device_id=(me_c, j), device_id_type=MESH)

    def line_copy(block, j, target, send_sem, mine_too=False):
        place = rfbuf.at[block, :, piece(j)]
        return pltpu.make_async_remote_copy(
            src_ref=rf_ref.at[:, me_bin] if mine_too else place, dst_ref=place,
            send_sem=send_sem, recv_sem=line_recv.at[block * nf + j],
            device_id=(target, me_f), device_id_type=MESH)

    def own_copy(j, offset, mine_too=False):
        slot = offset + REACH - (offset > 0)
        return line_copy(me_c, j, me_c + offset, line_send.at[slot * nf + j], mine_too)

    def relay_copy(block, j):
        target = jnp.where(block < me_c, me_c + 1, me_c - 1)
        return line_copy(block, j, target, relay_send.at[block * nf + j])

    def there(offset):
        return me_c + offset < nc if offset > 0 else me_c + offset >= 0

    def send_far(j, mine_too=False):
        for offset in range(REACH, 0, -1):
            for signed in (offset, -offset):
                farther = signed + (1 if signed > 0 else -1)
                condition = there(signed)
                if offset < REACH:
                    condition = jnp.logical_and(condition, jnp.logical_not(there(farther)))

                @pl.when(condition)
                def _():
                    own_copy(j, signed, mine_too).start()

    def send_near(j, mine_too=False):
        for offset in range(REACH - 1, 0, -1):
            for signed in (offset, -offset):
                @pl.when(there(signed + (1 if signed > 0 else -1)))
                def _():
                    own_copy(j, signed, mine_too).start()

    if_first(lambda: send_far(me_f, True))
    base_f = me_f - lax.rem(me_f, 2)
    for parity in (0, 1):
        for k in range(0, nf, 2):
            j = lax.rem(base_f + k, nf) + parity
            if k == 0:
                @pl.when(j != me_f)
                def _():
                    plane_copy(j).start()
            else:
                plane_copy(j).start()

    inverse = 2.0 / math.sqrt(chans)
    for load in loads:
        load.wait()
    vox[...] = vox_ref[:, pl.ds(pl.multiple_of(me_sub * vd, LANES), vd)].astype(F32)
    for axis in range(3):
        for base in range(0, chans, LANES):
            row = elem_ref[axis:axis + 1, base:base + LANES].astype(F32)
            elem[axis, base:base + LANES, :] = jnp.broadcast_to(row, (LANES, LANES)).T
    wavenum = (32.0 + sub_ref[me_bin].astype(F32)) / 64.0

    tall = cl // TALL
    steps = nc * tall

    def make_operator(low, high):
        @pl.loop(low, high)
        def _(step):
            block = lax.rem(me_c + lax.div(step, tall), nc)
            place = pl.ds(pl.multiple_of(block * cl + lax.rem(step, tall) * TALL, TALL), TALL)
            ex, ey, ez = elem[0, place, :], elem[1, place, :], elem[2, place, :]
            for base in range(0, vd, LANES):
                lanes = slice(base, base + LANES)
                vz = vox[2:3, lanes]
                dx, dy, dz = vox[0:1, lanes] - ex, vox[1:2, lanes] - ey, vz - ez
                square = dx * dx + dy * dy + dz * dz
                inv = lax.rsqrt(square)
                turns = wavenum * (vz + square * inv)
                turns = turns - ((turns + ROUND) - ROUND)
                z = turns * turns
                sine = turns * horner(SIN_POLY, z)
                cosine = horner(COS_POLY, z)
                twice = dz * inverse * inv
                oper[0, place, lanes] = (twice * (0.5 - sine * sine)).astype(BF16)
                oper[1, place, lanes] = (twice * sine * cosine).astype(BF16)

    def multiply_step(block, step, first=False, last=False):
        place = pl.ds(pl.multiple_of(block * cl, cl), cl)
        real, imag = rfbuf[block, 0], rfbuf[block, 1]
        left = jnp.concatenate(
            [jnp.concatenate([real, imag], axis=1), jnp.concatenate([imag, -real], axis=1)], axis=0)
        lanes = pl.ds(pl.multiple_of(step * width, width), width)
        value = dot(left, jnp.concatenate([oper[0, place, lanes], oper[1, place, lanes]], axis=0))
        if not first:
            value = value + acc[:, lanes]
        if last:
            vols[:, lanes] = value.astype(BF16)
        else:
            acc[:, lanes] = value

    def multiply(block, first=False, last=False):
        @pl.loop(0, halves)
        def _(step):
            multiply_step(block, step, first, last)

    def passed_on(block):
        right = jnp.logical_and(me_c - block >= REACH, me_c < nc - 1)
        return jnp.logical_or(right, jnp.logical_and(block - me_c >= REACH, me_c > 0))

    begin = steps // 8
    portion = (steps - begin) * 3 // 8 // (nf - 1)
    rest = begin + portion * (nf - 1)

    def let_go():
        pl.semaphore_signal(go_sem, inc=1, device_id=(me_c, me_f + 1), device_id_type=MESH)

    def run_second():
        make_operator(0, steps)

        @pl.loop(1, nf)
        def _(k):
            plane_arrival(partner(k)).wait_recv()

        own.wait()
        multiply(me_c, first=True)
        pl.semaphore_wait(go_sem, 1)

        @pl.loop(0, nf)
        def _(k):
            send_far(partner(k))

        @pl.loop(0, nf)
        def _(k):
            send_near(partner(k))

    def run_first():
        make_operator(0, begin)

        @pl.loop(1, nf)
        def _(k):
            j = partner(k)
            plane_arrival(j).wait_recv()
            send_far(j)
            make_operator(begin + (k - 1) * portion, begin + k * portion)

        send_near(me_f, True)

        @pl.loop(1, nf)
        def _(k):
            send_near(partner(k))

        own.wait()

    if stagger:
        pl.when(second)(run_second)
    if_first(run_first)

    @pl.loop(REACH, nc - 1)
    def _(hop):
        block = jnp.where(me_c >= hop, me_c - hop, me_c + hop)
        other = jnp.where(me_c >= hop, me_c + hop, nc)

        @pl.loop(0, nf)
        def _(k):
            j = partner(k)
            for which in (block, other):
                @pl.when(jnp.logical_and(which < nc, passed_on(which)))
                def _():
                    relay_copy(which, j).wait_recv()
                    relay_copy(which, j).start()

            def early():
                @pl.when(k < halves)
                def _():
                    make_operator(rest + lax.div((steps - rest) * k, halves), rest + lax.div((steps - rest) * (k + 1), halves))

                @pl.when(k >= halves)
                def _():
                    multiply_step(me_c, k - halves, first=True)

            if_first(early, hop == REACH)
            if stagger:
                if_first(let_go, hop == REACH, k == GO_AT * nf // 8)

    if nc <= REACH + 1:
        if_first(lambda: make_operator(rest, steps))
        if_first(lambda: multiply(me_c, first=True))
        if stagger:
            if_first(let_go)

    lower = 2 * me_c < nc
    depth = jnp.where(lower, me_c, nc - 1 - me_c)

    def block_in_turn(turn):
        place = jnp.where(turn <= depth, depth - turn, nc + depth - turn)
        place = jnp.where(depth == 0, turn, place)
        return jnp.where(lower, place, nc - 1 - place)

    def arrive(block):
        @pl.when(jnp.logical_not(passed_on(block)))
        def _():
            @pl.loop(0, nf)
            def _(k):
                j = partner(k)
                line_copy(block, j, block, relay_send.at[block * nf + j]).wait_recv()

    @pl.loop(1, nc - 1)
    def _(turn):
        block = block_in_turn(turn)
        arrive(block)
        multiply(block)

    arrive(block_in_turn(nc - 1))
    multiply(block_in_turn(nc - 1), last=True)

    real, imag = vols[:frames, :], vols[frames:, :]
    both = jnp.concatenate([real, imag], axis=1)
    gram_re = dot_nt(both, both)
    gram_im = dot_nt(jnp.concatenate([real, -imag], axis=1), jnp.concatenate([imag, real], axis=1))
    across = lax.broadcasted_iota(jnp.int32, (frames, frames), 1)
    down = lax.broadcasted_iota(jnp.int32, (frames, frames), 0)
    part[...] = jnp.where(down <= across, gram_re, gram_im).astype(BF16)

    members = [(c, t) for c in range(nc) for t in range(share)]

    def device(member):
        return member[0], me_bin * share + member[1]

    def is_me(member):
        return jnp.logical_and(me_c == member[0], me_sub == member[1])

    def half(index):
        return pl.ds(index * rows, rows)

    def scatter(index, source=None):
        origin = me_c * share + me_sub if source is None else members.index(source)
        return pltpu.make_async_remote_copy(
            src_ref=part.at[half(index)], dst_ref=slabs.at[origin],
            send_sem=rs_send.at[index], recv_sem=rs_recv.at[origin],
            device_id=device(owners[index]), device_id_type=MESH)

    def gather(index, member):
        place = total.at[half(index)]
        return pltpu.make_async_remote_copy(
            src_ref=place, dst_ref=place, send_sem=ag_send.at[members.index(member)], recv_sem=ag_recv.at[index],
            device_id=device(member), device_id_type=MESH)

    upper_half = 2 * me_c >= nc
    for turn in range(2):
        for index in range(2):
            across_line = upper_half if index == 0 else jnp.logical_not(upper_half)
            chosen = across_line if turn == 0 else jnp.logical_not(across_line)

            @pl.when(jnp.logical_and(chosen, jnp.logical_not(is_me(owners[index]))))
            def _():
                scatter(index).start()
    for index in range(2):
        @pl.when(is_me(owners[index]))
        def _():
            others = sorted(
                (m for m in members if m != owners[index]), key=lambda m: abs(m[0] - owners[index][0]))
            summed = part[half(index), :].astype(F32)
            for member in others:
                scatter(index, member).wait_recv()
                summed = summed + slabs[members.index(member)].astype(F32)
            total[half(index), :] = summed.astype(BF16)
            for member in others[::-1]:
                gather(index, member).start()
    for index in range(2):
        @pl.when(jnp.logical_not(is_me(owners[index])))
        def _():
            gather(index, owners[index]).wait_recv()

    packed = total[...].astype(F32)
    turned = packed.T
    same = down == across
    g_re = jnp.where(down <= across, packed, turned)
    g_im = jnp.where(down > across, packed, jnp.where(same, 0.0, -turned))
    squares = packed * packed
    squares = jnp.where(same, squares, squares + squares)
    squares = jnp.sum(jnp.sum(squares, axis=0, keepdims=True), axis=1, keepdims=True)
    factor = 4.0 / jnp.sqrt(squares + EPSILON)
    first = jnp.concatenate([g_re, g_im], axis=1).astype(BF16)
    below = jnp.concatenate([-g_im, g_re], axis=1).astype(BF16)
    rhs = jnp.concatenate([first, below], axis=0)
    second_power = dot(first, rhs)
    high = second_power.astype(BF16)
    low = (second_power - high.astype(F32)).astype(BF16)
    third_power = dot(high, rhs) + dot(low, rhs)
    poly = factor * (factor * (0.3 * second_power - (0.03 * factor) * third_power) - first.astype(F32))
    h_re = (jnp.where(same, 1.0, 0.0) + poly[:, :frames]).astype(BF16)
    h_im = poly[:, frames:].astype(BF16)
    hmat[:frames, :frames] = h_re
    hmat[:frames, frames:] = h_im
    hmat[frames:, :frames] = -h_im
    hmat[frames:, frames:] = h_re

    def out_copy(j, chunk):
        lanes = pl.ds(chunk * span, span)
        return pltpu.make_async_remote_copy(
            src_ref=sent.at[:, piece(j), lanes], dst_ref=out_ref.at[me_f, :, :, lanes],
            send_sem=out_send.at[chunk * nf + j], recv_sem=out_recv.at[chunk * nf + me_f],
            device_id=(me_c, j), device_id_type=MESH)

    chunks = out_own.shape[0]
    span = vd // chunks
    lhs = hmat[...]
    for chunk in range(chunks):
        lanes = pl.ds(chunk * span, span)
        value = dot(lhs, vols[:, lanes]).astype(BF16)
        sent[0, :, lanes] = value[:frames]
        sent[1, :, lanes] = value[frames:]
        for k in range(nf - 1, 0, -1):
            out_copy(partner(k), chunk).start()
        pltpu.make_async_copy(sent.at[:, mine, lanes], out_ref.at[me_f, :, :, lanes], out_own.at[chunk]).start()

    @pl.loop(1, nf)
    def _(k):
        plane_copy(partner(k)).wait_send()

    @pl.loop(0, nf)
    def _(j):
        for offset in range(1, REACH + 1):
            for signed in (offset, -offset):
                @pl.when(there(signed))
                def _():
                    own_copy(j, signed).wait_send()

        @pl.loop(0, nc)
        def _(block):
            @pl.when(passed_on(block))
            def _():
                relay_copy(block, j).wait_send()

    for index in range(2):
        @pl.when(jnp.logical_not(is_me(owners[index])))
        def _():
            scatter(index).wait_send()

        @pl.when(is_me(owners[index]))
        def _():
            for member in members:
                if member != owners[index]:
                    gather(index, member).wait_send()
    for chunk in range(chunks):
        lanes = pl.ds(chunk * span, span)
        pltpu.make_async_copy(sent.at[:, mine, lanes], out_ref.at[me_f, :, :, lanes], out_own.at[chunk]).wait()

        @pl.loop(1, nf)
        def _(k):
            j = partner(k)
            out_copy(j, chunk).wait_send()
            pltpu.make_async_remote_copy(
                src_ref=sent.at[:, mine, lanes], dst_ref=out_ref.at[j, :, :, lanes],
                send_sem=out_send.at[chunk * nf + j], recv_sem=out_recv.at[chunk * nf + j],
                device_id=(me_c, j), device_id_type=MESH).wait_recv()


def shards(nc, nf, rf_data, elem_pos, vox_pos, subbands):
    nbins, fl, cl = rf_data.shape[1:]
    frames = fl * nf
    chans = cl * nc
    share = nf // nbins
    vl = vox_pos.shape[1]
    vd = vl // share
    group = nc * share
    chunks = 4
    dma = pltpu.SemaphoreType.DMA
    inputs = [pltpu.with_memory_space_constraint(x, pltpu.HBM) for x in (rf_data, elem_pos, vox_pos, subbands)]
    received = pl.pallas_call(
        functools.partial(kernel, nc, nf, nbins),
        out_shape=pltpu.VMEM((nf, 2, fl, vd), BF16),
        in_specs=[pl.BlockSpec(memory_space=pl.ANY)] * 4,
        out_specs=pl.BlockSpec(memory_space=pl.ANY),
        scratch_shapes=[
            pltpu.VMEM((nc, 2, frames, cl), BF16),
            pltpu.VMEM(elem_pos.shape, elem_pos.dtype),
            pltpu.VMEM(vox_pos.shape, vox_pos.dtype),
            pltpu.SMEM(subbands.shape, subbands.dtype),
            dma((3,)),
            pltpu.VMEM((3, chans, LANES), F32),
            pltpu.VMEM((3, vd), F32),
            pltpu.VMEM((2, chans, vd), BF16),
            pltpu.VMEM((2 * frames, vd), F32),
            pltpu.VMEM((2 * frames, vd), BF16),
            pltpu.VMEM((frames, frames), BF16),
            pltpu.VMEM((group, frames // 2, frames), BF16),
            pltpu.VMEM((frames, frames), BF16),
            pltpu.VMEM((2 * frames, 2 * frames), BF16),
            pltpu.VMEM((2, frames, vd), BF16),
            pltpu.SemaphoreType.REGULAR, dma, dma((nf,)), dma((nf,)),
            dma((2 * REACH * nf,)), dma((nc * nf,)), dma((nc * nf,)),
            dma((2,)), dma((group,)), dma((group,)), dma((2,)),
            dma((chunks,)), dma((chunks * nf,)), dma((chunks * nf,)),
        ],
        compiler_params=pltpu.CompilerParams(
            collective_id=0, has_side_effects=True, vmem_limit_bytes=40 * 2**20),
    )(*inputs)
    received = received.reshape(nbins, share, 2, fl, vd)
    return jnp.transpose(received, (3, 2, 0, 1, 4)).reshape(fl, 2, nbins, vl)


def solution(mesh):
    return jax.shard_map(
        functools.partial(shards, mesh.shape["chan"], mesh.shape["frame"]),
        mesh=mesh,
        in_specs=(P(None, None, "frame", "chan"), P(), P(None, "chan"), P()),
        out_specs=P("frame", None, None, "chan"),
        check_vma=False,
    )
```

```python
import functools
import math

import jax
import jax.numpy as jnp
from jax import lax
from jax.experimental import pallas as pl
from jax.experimental.pallas import tpu as pltpu
from jax.sharding import PartitionSpec as P

EPSILON = 1e-06
MESH = pl.DeviceIdType.MESH
F32 = jnp.float32
BF16 = jnp.bfloat16
SIN_POLY = (3.1415820121765137, -5.167142868041992, 2.5418989658355713, -0.5546361804008484)
BELOW_ONE = 1.0 - 2e-6
LANES = 128
ROUND = 12582912.0
TALL = 32
REACH = 2
GO_AT = 7
SECOND_REACH = 1


def horner(coefs, z):
    value = coefs[-1] * z + coefs[-2]
    for coef in coefs[-3::-1]:
        value = value * z + coef
    return value


def dot(a, b):
    return jnp.dot(a, b, preferred_element_type=F32)


def dot_nt(a, b):
    return lax.dot_general(a, b, (((1,), (1,)), ((), ())), preferred_element_type=F32)


def kernel(
    nc, nf, nbins,
    rf_ref, elem_hbm, vox_hbm, sub_hbm, out_ref,
    rfbuf, elem_ref, vox_ref, sub_ref, in_sem, elem, heights, vox, squares, oper, acc, vols, part, slabs, total, hmat, sent,
    go_sem, own_sem, plane_send, plane_recv, line_send, relay_send, line_recv,
    rs_send, rs_recv, ag_send, ag_recv, out_own, out_send, out_recv,
):
    share = nf // nbins
    stagger = share == 1 and nf % 2 == 0
    frames = rfbuf.shape[2]
    cl = rfbuf.shape[3]
    chans = nc * cl
    vd = vols.shape[1]
    fl = frames // nf
    rows = frames // 2
    owners = ((nc // 2 - 1, 0), (nc // 2, 0))
    me_c = lax.axis_index("chan")
    me_f = lax.axis_index("frame")
    me_bin = lax.div(me_f, share)
    me_sub = lax.rem(me_f, share)
    second = lax.rem(me_f, 2) == 1
    first_core = jnp.logical_not(second)
    def partner(k):
        j = 0
        bit = 1
        while bit < nf:
            a = lax.rem(lax.div(me_f, bit), 2)
            b = k // bit % 2 if isinstance(k, int) else lax.rem(lax.div(k, bit), 2)
            j = j + bit * (a + b - 2 * a * b)
            bit *= 2
        return j

    reach = jnp.where(second, SECOND_REACH, REACH) if stagger else REACH

    def if_first(run, *conditions):
        for condition in conditions + ((first_core,) if stagger else ()):
            run = functools.partial(pl.when(condition), run)
        run()

    def piece(j):
        return pl.ds(pl.multiple_of(j * fl, fl), fl)

    barrier = pltpu.get_barrier_semaphore()
    for k in range(1, nf):
        pl.semaphore_signal(barrier, inc=1, device_id=(me_c, partner(k)), device_id_type=MESH)
    for k in range(1, nc):
        for s in range(share):
            other = (lax.rem(me_c + k, nc), me_bin * share + s)
            pl.semaphore_signal(barrier, inc=1, device_id=other, device_id_type=MESH)

    mine = piece(me_f)
    loads = [
        pltpu.make_async_copy(source, place, in_sem.at[index])
        for index, (source, place) in enumerate(
            ((elem_hbm, elem_ref), (vox_hbm, vox_ref), (sub_hbm, sub_ref)))
    ]
    for load in loads:
        load.start()
    own = pltpu.make_async_copy(rf_ref.at[:, me_bin], rfbuf.at[me_c, :, mine], own_sem)
    own.start()
    pl.semaphore_wait(barrier, nf - 1 + (nc - 1) * share)

    def plane_copy(j):
        return pltpu.make_async_remote_copy(
            src_ref=rf_ref.at[:, lax.div(j, share)], dst_ref=rfbuf.at[me_c, :, mine],
            send_sem=plane_send.at[j], recv_sem=plane_recv.at[me_f],
            device_id=(me_c, j), device_id_type=MESH)

    def plane_arrival(j):
        return pltpu.make_async_remote_copy(
            src_ref=rf_ref.at[:, 0], dst_ref=rfbuf.at[me_c, :, piece(j)], send_sem=plane_send.at[j],
            recv_sem=plane_recv.at[j], device_id=(me_c, j), device_id_type=MESH)

    def line_copy(block, j, target, send_sem, mine_too=False):
        place = rfbuf.at[block, :, piece(j)]
        return pltpu.make_async_remote_copy(
            src_ref=rf_ref.at[:, me_bin] if mine_too else place, dst_ref=place,
            send_sem=send_sem, recv_sem=line_recv.at[block * nf + j],
            device_id=(target, me_f), device_id_type=MESH)

    def own_copy(j, offset, mine_too=False):
        slot = offset + REACH - (offset > 0)
        return line_copy(me_c, j, me_c + offset, line_send.at[slot * nf + j], mine_too)

    def relay_copy(block, j):
        target = jnp.where(block < me_c, me_c + 1, me_c - 1)
        return line_copy(block, j, target, relay_send.at[block * nf + j])

    def there(offset):
        return me_c + offset < nc if offset > 0 else me_c + offset >= 0

    def send_far(j, mine_too=False):
        for offset in range(REACH, 0, -1):
            for signed in (offset, -offset):
                farther = signed + (1 if signed > 0 else -1)
                condition = there(signed)
                if offset < REACH:
                    condition = jnp.logical_and(condition, jnp.logical_not(there(farther)))

                @pl.when(condition)
                def _():
                    own_copy(j, signed, mine_too).start()

    def send_near(j, mine_too=False):
        for offset in range(REACH - 1, 0, -1):
            for signed in (offset, -offset):
                @pl.when(there(signed + (1 if signed > 0 else -1)))
                def _():
                    own_copy(j, signed, mine_too).start()

    if_first(lambda: send_far(me_f, True))
    base_f = me_f - lax.rem(me_f, 2)
    for parity in (0, 1):
        for k in range(0, nf, 2):
            j = lax.rem(base_f + k, nf) + parity
            if k == 0:
                @pl.when(j != me_f)
                def _():
                    plane_copy(j).start()
            else:
                plane_copy(j).start()

    scale = 2.0 / math.sqrt(chans)
    sin_poly = [coef * math.sqrt(scale) * BELOW_ONE for coef in SIN_POLY]
    for load in loads:
        load.wait()
    wavenum = (32.0 + sub_ref[me_bin].astype(F32)) / 64.0
    voxels = vox_ref[:, pl.ds(pl.multiple_of(me_sub * vd, LANES), vd)].astype(F32)
    vx, vy, vz = voxels[0:1], voxels[1:2], voxels[2:3]
    vox[...] = vz * wavenum
    kind = lax.broadcasted_iota(jnp.int32, (8, vd), 0)
    terms = jnp.where(kind == 0, vx, jnp.where(kind == 1, vy, vz)) * -2.0
    terms = jnp.where(kind < 3, terms, jnp.where(kind == 3, vx * vx + vy * vy + vz * vz, 1.0)) * (wavenum * wavenum)
    terms = jnp.where(kind < 6, terms, 0.0)
    parts = []
    for _ in range(3):
        parts.append(terms.astype(BF16).astype(F32))
        terms = terms - parts[-1]
    right = jnp.concatenate(parts + [jnp.zeros((LANES - 24, vd), F32)], axis=0).astype(BF16)
    kind = lax.broadcasted_iota(jnp.int32, (8, LANES), 0)
    for base in range(0, chans, LANES):
        points = elem_ref[:, base:base + LANES]
        ex, ey, ez = points[0:1], points[1:2], points[2:3]
        norm = ex * ex + ey * ey + ez * ez
        low = jnp.bitwise_and(norm, 15)
        facts = jnp.where(kind == 0, ex, jnp.where(kind == 1, ey, jnp.where(kind == 2, ez, 1)))
        facts = jnp.where(kind < 4, facts, jnp.where(kind == 4, norm - low, jnp.where(kind == 5, low, 0))).astype(F32)
        facts = jnp.concatenate([facts, facts, facts, jnp.zeros((LANES - 24, LANES), F32)], axis=0)
        elem[base:base + LANES, :] = facts.T.astype(BF16)
        heights[base:base + LANES, :] = jnp.broadcast_to(ez.astype(F32) * wavenum, (LANES, LANES)).T
    squares[...] = dot(elem[...], right)

    tall = cl // TALL
    steps = nc * tall

    def make_operator(low, high):
        @pl.loop(low, high)
        def _(step):
            block = lax.rem(me_c + lax.div(step, tall), nc)
            place = pl.ds(pl.multiple_of(block * cl + lax.rem(step, tall) * TALL, TALL), TALL)
            ez = heights[place, :]
            for base in range(0, vd, LANES):
                lanes = slice(base, base + LANES)
                vz, square = vox[:, lanes], squares[place, lanes]
                inv = lax.rsqrt(square)
                turns = vz + square * inv
                turns = turns - ((turns + ROUND) - ROUND)
                sine = turns * horner(sin_poly, turns * turns)
                rest = scale - sine * sine
                cosine = rest * lax.rsqrt(rest)
                twice = (vz - ez) * inv
                oper[0, place, lanes] = (twice * (rest - 0.5 * scale)).astype(BF16)
                oper[1, place, lanes] = (twice * sine * cosine).astype(BF16)

    def multiply(block, first=False, last=False, part_of=None):
        place = pl.ds(pl.multiple_of(block * cl, cl), cl)
        right = jnp.concatenate([oper[0, place, :], oper[1, place, :]], axis=0)
        if part_of is None:
            real, imag = rfbuf[block, 0], rfbuf[block, 1]
            wheres = (slice(0, 2 * frames),)
        else:
            some = pl.ds(pl.multiple_of(part_of * rows, rows), rows)
            real, imag = rfbuf[block, 0, some, :], rfbuf[block, 1, some, :]
            wheres = (some, pl.ds(pl.multiple_of(frames + part_of * rows, rows), rows))
        left = jnp.concatenate(
            [jnp.concatenate([real, imag], axis=1), jnp.concatenate([imag, -real], axis=1)], axis=0)
        value = dot(left, right)
        for index, where in enumerate(wheres):
            some = value if part_of is None else value[index * rows:(index + 1) * rows]
            if not first:
                some = some + acc[where, :]
            if last:
                vols[where, :] = some.astype(BF16)
            else:
                acc[where, :] = some

    def passed_on(block):
        right = jnp.logical_and(me_c - block >= reach, me_c < nc - 1)
        return jnp.logical_or(right, jnp.logical_and(block - me_c >= reach, me_c > 0))

    begin = steps // 8
    portion = 0
    rest = begin + portion * (nf - 1)
    later = rest + (steps - rest) * 6 // 8

    def let_go():
        pl.semaphore_signal(go_sem, inc=1, device_id=(me_c, me_f + 1), device_id_type=MESH)

    def run_second():
        make_operator(0, steps)

        @pl.loop(1, nf)
        def _(k):
            plane_arrival(partner(k)).wait_recv()

        own.wait()
        multiply(me_c, first=True)
        pl.semaphore_wait(go_sem, 1)

        @pl.loop(0, nf)
        def _(k):
            j = partner(k)
            for offset in (1, -1):
                pl.when(there(offset))(own_copy(j, offset).start)

    def run_first():
        make_operator(0, begin)

        @pl.loop(1, nf)
        def _(k):
            j = partner(k)
            plane_arrival(j).wait_recv()
            send_far(j)
            if portion:
                make_operator(begin + (k - 1) * portion, begin + k * portion)

        send_near(me_f, True)

        @pl.loop(1, nf)
        def _(k):
            send_near(partner(k))

        own.wait()

    if stagger:
        pl.when(second)(run_second)
    if_first(run_first)

    @pl.loop(reach, nc - 1)
    def _(hop):
        block = jnp.where(me_c >= hop, me_c - hop, me_c + hop)
        other = jnp.where(me_c >= hop, me_c + hop, nc)

        @pl.loop(0, nf)
        def _(k):
            j = partner(k)
            for which in (block, other):
                @pl.when(jnp.logical_and(which < nc, passed_on(which)))
                def _():
                    relay_copy(which, j).wait_recv()
                    relay_copy(which, j).start()

            def early():
                make_operator(rest + lax.div((later - rest) * k, nf), rest + lax.div((later - rest) * (k + 1), nf))

            if_first(early, hop == REACH)
            if stagger:
                if_first(let_go, hop == REACH, k == GO_AT * nf // 8)

    if nc <= REACH + 1:
        if_first(lambda: make_operator(rest, later))
        if stagger:
            if_first(let_go)
    if_first(lambda: make_operator(later, steps))
    if_first(lambda: multiply(me_c, first=True))

    lower = 2 * me_c < nc
    depth = jnp.where(lower, me_c, nc - 1 - me_c)

    def block_in_turn(turn):
        place = jnp.where(turn <= depth, depth - turn, nc + depth - turn)
        place = jnp.where(depth == 0, turn, place)
        return jnp.where(lower, place, nc - 1 - place)

    def arrive(block, low=0, high=nf):
        @pl.when(jnp.logical_not(passed_on(block)))
        def _():
            @pl.loop(low, high)
            def _(k):
                j = partner(k)
                line_copy(block, j, block, relay_send.at[block * nf + j]).wait_recv()

    @pl.loop(1, nc - 1)
    def _(turn):
        block = block_in_turn(turn)
        arrive(block)
        multiply(block)

    block = block_in_turn(nc - 1)
    near = lax.div(me_f, nf // 2)
    arrive(block, 0, nf // 2)
    multiply(block, last=True, part_of=near)
    arrive(block, nf // 2, nf)
    multiply(block, last=True, part_of=1 - near)

    real, imag = vols[:frames, :], vols[frames:, :]
    both = jnp.concatenate([real, imag], axis=1)
    gram_re = dot_nt(both, both)
    gram_im = dot_nt(jnp.concatenate([real, -imag], axis=1), jnp.concatenate([imag, real], axis=1))
    across = lax.broadcasted_iota(jnp.int32, (frames, frames), 1)
    down = lax.broadcasted_iota(jnp.int32, (frames, frames), 0)
    part[...] = jnp.where(down <= across, gram_re, gram_im).astype(BF16)

    members = [(c, t) for c in range(nc) for t in range(share)]

    def device(member):
        return member[0], me_bin * share + member[1]

    def is_me(member):
        return jnp.logical_and(me_c == member[0], me_sub == member[1])

    def half(index):
        return pl.ds(index * rows, rows)

    def scatter(index, source=None):
        origin = me_c * share + me_sub if source is None else members.index(source)
        return pltpu.make_async_remote_copy(
            src_ref=part.at[half(index)], dst_ref=slabs.at[origin],
            send_sem=rs_send.at[index], recv_sem=rs_recv.at[origin],
            device_id=device(owners[index]), device_id_type=MESH)

    def gather(index, member):
        place = total.at[half(index)]
        return pltpu.make_async_remote_copy(
            src_ref=place, dst_ref=place, send_sem=ag_send.at[members.index(member)], recv_sem=ag_recv.at[index],
            device_id=device(member), device_id_type=MESH)

    upper_half = 2 * me_c >= nc
    for turn in range(2):
        for index in range(2):
            across_line = upper_half if index == 0 else jnp.logical_not(upper_half)
            chosen = across_line if turn == 0 else jnp.logical_not(across_line)

            @pl.when(jnp.logical_and(chosen, jnp.logical_not(is_me(owners[index]))))
            def _():
                scatter(index).start()
    for index in range(2):
        @pl.when(is_me(owners[index]))
        def _():
            others = sorted(
                (m for m in members if m != owners[index]), key=lambda m: abs(m[0] - owners[index][0]))
            summed = part[half(index), :].astype(F32)
            for member in others:
                scatter(index, member).wait_recv()
                summed = summed + slabs[members.index(member)].astype(F32)
            total[half(index), :] = summed.astype(BF16)
            for member in others[::-1]:
                gather(index, member).start()
    for index in range(2):
        @pl.when(jnp.logical_not(is_me(owners[index])))
        def _():
            gather(index, owners[index]).wait_recv()

    packed = total[...].astype(F32)
    turned = packed.T
    same = down == across
    g_re = jnp.where(down <= across, packed, turned)
    g_im = jnp.where(down > across, packed, jnp.where(same, 0.0, -turned))
    norm = packed * packed
    norm = jnp.where(same, norm, norm + norm)
    norm = jnp.sum(jnp.sum(norm, axis=0, keepdims=True), axis=1, keepdims=True)
    factor = 4.0 / jnp.sqrt(norm + EPSILON)
    first = jnp.concatenate([g_re, g_im], axis=1).astype(BF16)
    below = jnp.concatenate([-g_im, g_re], axis=1).astype(BF16)
    rhs = jnp.concatenate([first, below], axis=0)
    second_power = dot(first, rhs)
    high = second_power.astype(BF16)
    low = (second_power - high.astype(F32)).astype(BF16)
    third_power = dot(high, rhs) + dot(low, rhs)
    poly = factor * (factor * (0.3 * second_power - (0.03 * factor) * third_power) - first.astype(F32))
    h_re = (jnp.where(same, 1.0, 0.0) + poly[:, :frames]).astype(BF16)
    h_im = poly[:, frames:].astype(BF16)
    hmat[:frames, :frames] = h_re
    hmat[:frames, frames:] = h_im
    hmat[frames:, :frames] = -h_im
    hmat[frames:, frames:] = h_re

    def out_copy(j, chunk):
        lanes = pl.ds(chunk * span, span)
        return pltpu.make_async_remote_copy(
            src_ref=sent.at[:, piece(j), lanes], dst_ref=out_ref.at[me_f, :, :, lanes],
            send_sem=out_send.at[chunk * nf + j], recv_sem=out_recv.at[chunk * nf + me_f],
            device_id=(me_c, j), device_id_type=MESH)

    chunks = out_own.shape[0]
    span = vd // chunks
    lhs = hmat[...]
    for chunk in range(chunks):
        lanes = pl.ds(chunk * span, span)
        value = dot(lhs, vols[:, lanes]).astype(BF16)
        sent[0, :, lanes] = value[:frames]
        sent[1, :, lanes] = value[frames:]
        for k in range(nf - 1, 0, -1):
            out_copy(partner(k), chunk).start()
        pltpu.make_async_copy(sent.at[:, mine, lanes], out_ref.at[me_f, :, :, lanes], out_own.at[chunk]).start()

    @pl.loop(1, nf)
    def _(k):
        plane_copy(partner(k)).wait_send()

    @pl.loop(0, nf)
    def _(j):
        for offset in range(1, REACH + 1):
            for signed in (offset, -offset):
                sent_it = there(signed) if offset == 1 else jnp.logical_and(there(signed), reach >= offset)

                @pl.when(sent_it)
                def _():
                    own_copy(j, signed).wait_send()

        @pl.loop(0, nc)
        def _(block):
            @pl.when(passed_on(block))
            def _():
                relay_copy(block, j).wait_send()

    for index in range(2):
        @pl.when(jnp.logical_not(is_me(owners[index])))
        def _():
            scatter(index).wait_send()

        @pl.when(is_me(owners[index]))
        def _():
            for member in members:
                if member != owners[index]:
                    gather(index, member).wait_send()
    for chunk in range(chunks):
        lanes = pl.ds(chunk * span, span)
        pltpu.make_async_copy(sent.at[:, mine, lanes], out_ref.at[me_f, :, :, lanes], out_own.at[chunk]).wait()

        @pl.loop(1, nf)
        def _(k):
            j = partner(k)
            out_copy(j, chunk).wait_send()
            pltpu.make_async_remote_copy(
                src_ref=sent.at[:, mine, lanes], dst_ref=out_ref.at[j, :, :, lanes],
                send_sem=out_send.at[chunk * nf + j], recv_sem=out_recv.at[chunk * nf + j],
                device_id=(me_c, j), device_id_type=MESH).wait_recv()


def shards(nc, nf, rf_data, elem_pos, vox_pos, subbands):
    nbins, fl, cl = rf_data.shape[1:]
    frames = fl * nf
    chans = cl * nc
    share = nf // nbins
    vl = vox_pos.shape[1]
    vd = vl // share
    group = nc * share
    chunks = 4
    dma = pltpu.SemaphoreType.DMA
    inputs = [pltpu.with_memory_space_constraint(x, pltpu.HBM) for x in (rf_data, elem_pos, vox_pos, subbands)]
    received = pl.pallas_call(
        functools.partial(kernel, nc, nf, nbins),
        out_shape=pltpu.VMEM((nf, 2, fl, vd), BF16),
        in_specs=[pl.BlockSpec(memory_space=pl.ANY)] * 4,
        out_specs=pl.BlockSpec(memory_space=pl.ANY),
        scratch_shapes=[
            pltpu.VMEM((nc, 2, frames, cl), BF16),
            pltpu.VMEM(elem_pos.shape, elem_pos.dtype),
            pltpu.VMEM(vox_pos.shape, vox_pos.dtype),
            pltpu.SMEM(subbands.shape, subbands.dtype),
            dma((3,)),
            pltpu.VMEM((chans, LANES), BF16),
            pltpu.VMEM((chans, LANES), F32),
            pltpu.VMEM((1, vd), F32),
            pltpu.VMEM((chans, vd), F32),
            pltpu.VMEM((2, chans, vd), BF16),
            pltpu.VMEM((2 * frames, vd), F32),
            pltpu.VMEM((2 * frames, vd), BF16),
            pltpu.VMEM((frames, frames), BF16),
            pltpu.VMEM((group, frames // 2, frames), BF16),
            pltpu.VMEM((frames, frames), BF16),
            pltpu.VMEM((2 * frames, 2 * frames), BF16),
            pltpu.VMEM((2, frames, vd), BF16),
            pltpu.SemaphoreType.REGULAR, dma, dma((nf,)), dma((nf,)),
            dma((2 * REACH * nf,)), dma((nc * nf,)), dma((nc * nf,)),
            dma((2,)), dma((group,)), dma((group,)), dma((2,)),
            dma((chunks,)), dma((chunks * nf,)), dma((chunks * nf,)),
        ],
        compiler_params=pltpu.CompilerParams(
            collective_id=0, has_side_effects=True, vmem_limit_bytes=40 * 2**20),
    )(*inputs)
    received = received.reshape(nbins, share, 2, fl, vd)
    return jnp.transpose(received, (3, 2, 0, 1, 4)).reshape(fl, 2, nbins, vl)


def solution(mesh):
    return jax.shard_map(
        functools.partial(shards, mesh.shape["chan"], mesh.shape["frame"]),
        mesh=mesh,
        in_specs=(P(None, None, "frame", "chan"), P(), P(None, "chan"), P()),
        out_specs=P("frame", None, None, "chan"),
        check_vma=False,
    )
```

```python
import functools
import math

import jax
import jax.numpy as jnp
from jax import lax
from jax.experimental import pallas as pl
from jax.experimental.pallas import tpu as pltpu
from jax.sharding import PartitionSpec as P

EPSILON = 1e-06
MESH = pl.DeviceIdType.MESH
F32 = jnp.float32
BF16 = jnp.bfloat16
SIN_POLY = (3.1415820121765137, -5.167142868041992, 2.5418989658355713, -0.5546361804008484)
BELOW_ONE = 1.0 - 2e-6
LANES = 128
ROUND = 12582912.0
TALL = 32
REACH = 2
GO_AT = 7
SECOND_REACH = 1


def horner(coefs, z):
    value = coefs[-1] * z + coefs[-2]
    for coef in coefs[-3::-1]:
        value = value * z + coef
    return value


def dot(a, b):
    return jnp.dot(a, b, preferred_element_type=F32)


def dot_nt(a, b):
    return lax.dot_general(a, b, (((1,), (1,)), ((), ())), preferred_element_type=F32)


def kernel(
    nc, nf, nbins,
    rf_ref, elem_hbm, vox_hbm, sub_hbm, out_ref,
    rfbuf, elem_ref, vox_ref, sub_ref, in_sem, elem, heights, vox, squares, oper, acc, vols, part, slabs, total, hmat, sent,
    met_sem, go_sem, own_sem, plane_send, plane_recv, line_send, relay_send, line_recv,
    rs_send, rs_recv, ag_send, ag_recv, out_own, out_send, out_recv,
):
    share = nf // nbins
    stagger = share == 1 and nf % 2 == 0
    frames = rfbuf.shape[2]
    cl = rfbuf.shape[3]
    chans = nc * cl
    vd = vols.shape[1]
    fl = frames // nf
    rows = frames // 2
    owners = ((nc // 2 - 1, 0), (nc // 2, 0))
    me_c = lax.axis_index("chan")
    me_f = lax.axis_index("frame")
    me_bin = lax.div(me_f, share)
    me_sub = lax.rem(me_f, share)
    second = lax.rem(me_f, 2) == 1
    first_core = jnp.logical_not(second)
    def partner(k):
        j = 0
        bit = 1
        while bit < nf:
            a = lax.rem(lax.div(me_f, bit), 2)
            b = k // bit % 2 if isinstance(k, int) else lax.rem(lax.div(k, bit), 2)
            j = j + bit * (a + b - 2 * a * b)
            bit *= 2
        return j

    reach = jnp.where(second, SECOND_REACH, REACH) if stagger else REACH

    def if_first(run, *conditions):
        for condition in conditions + ((first_core,) if stagger else ()):
            run = functools.partial(pl.when(condition), run)
        run()

    def piece(j):
        return pl.ds(pl.multiple_of(j * fl, fl), fl)

    base_f = me_f - lax.rem(me_f, 2)
    barrier = pltpu.get_barrier_semaphore()
    for step in range(2, nf, 2):
        pl.semaphore_signal(barrier, inc=1, device_id=(me_c, lax.rem(base_f + step, nf)), device_id_type=MESH)

    @pl.when(second)
    def _():
        pl.semaphore_signal(barrier, inc=1, device_id=(me_c, base_f), device_id_type=MESH)

    for step in range(1, nc):
        pl.semaphore_signal(barrier, inc=1, device_id=(lax.rem(me_c + step, nc), base_f + 1), device_id_type=MESH)

    mine = piece(me_f)
    loads = [
        pltpu.make_async_copy(source, place, in_sem.at[index])
        for index, (source, place) in enumerate(
            ((elem_hbm, elem_ref), (vox_hbm, vox_ref), (sub_hbm, sub_ref)))
    ]
    for load in loads:
        load.start()
    own = pltpu.make_async_copy(rf_ref.at[:, me_bin], rfbuf.at[me_c, :, mine], own_sem)
    own.start()

    @pl.when(first_core)
    def _():
        pl.semaphore_wait(barrier, nf - 1)
        pl.semaphore_signal(met_sem, inc=1, device_id=(me_c, base_f + 1), device_id_type=MESH)

    @pl.when(second)
    def _():
        pl.semaphore_wait(met_sem, 1)

    def plane_copy(j):
        return pltpu.make_async_remote_copy(
            src_ref=rf_ref.at[:, lax.div(j, share)], dst_ref=rfbuf.at[me_c, :, mine],
            send_sem=plane_send.at[j], recv_sem=plane_recv.at[me_f],
            device_id=(me_c, j), device_id_type=MESH)

    def plane_arrival(j):
        return pltpu.make_async_remote_copy(
            src_ref=rf_ref.at[:, 0], dst_ref=rfbuf.at[me_c, :, piece(j)], send_sem=plane_send.at[j],
            recv_sem=plane_recv.at[j], device_id=(me_c, j), device_id_type=MESH)

    def line_copy(block, j, target, send_sem, mine_too=False):
        place = rfbuf.at[block, :, piece(j)]
        return pltpu.make_async_remote_copy(
            src_ref=rf_ref.at[:, me_bin] if mine_too else place, dst_ref=place,
            send_sem=send_sem, recv_sem=line_recv.at[block * nf + j],
            device_id=(target, me_f), device_id_type=MESH)

    def own_copy(j, offset, mine_too=False):
        slot = offset + REACH - (offset > 0)
        return line_copy(me_c, j, me_c + offset, line_send.at[slot * nf + j], mine_too)

    def relay_copy(block, j):
        target = jnp.where(block < me_c, me_c + 1, me_c - 1)
        return line_copy(block, j, target, relay_send.at[block * nf + j])

    def there(offset):
        return me_c + offset < nc if offset > 0 else me_c + offset >= 0

    def send_far(j, mine_too=False):
        for offset in range(REACH, 0, -1):
            for signed in (offset, -offset):
                farther = signed + (1 if signed > 0 else -1)
                condition = there(signed)
                if offset < REACH:
                    condition = jnp.logical_and(condition, jnp.logical_not(there(farther)))

                @pl.when(condition)
                def _():
                    own_copy(j, signed, mine_too).start()

    def send_near(j, mine_too=False):
        for offset in range(REACH - 1, 0, -1):
            for signed in (offset, -offset):
                @pl.when(there(signed + (1 if signed > 0 else -1)))
                def _():
                    own_copy(j, signed, mine_too).start()

    for parity in (0, 1):
        for k in range(0, nf, 2):
            j = lax.rem(base_f + k, nf) + parity
            if k == 0:
                @pl.when(j != me_f)
                def _():
                    plane_copy(j).start()
            else:
                plane_copy(j).start()

    @pl.when(first_core)
    def _():
        pl.semaphore_wait(met_sem, 1)

    @pl.when(second)
    def _():
        pl.semaphore_wait(barrier, (nc - 1) * 2)
        pl.semaphore_signal(met_sem, inc=1, device_id=(me_c, base_f), device_id_type=MESH)

    if_first(lambda: send_far(me_f, True))

    scale = 2.0 / math.sqrt(chans)
    sin_poly = [coef * math.sqrt(scale) * BELOW_ONE for coef in SIN_POLY]
    for load in loads:
        load.wait()
    wavenum = (32.0 + sub_ref[me_bin].astype(F32)) / 64.0
    voxels = vox_ref[:, pl.ds(pl.multiple_of(me_sub * vd, LANES), vd)].astype(F32)
    vx, vy, vz = voxels[0:1], voxels[1:2], voxels[2:3]
    vox[...] = vz * wavenum
    kind = lax.broadcasted_iota(jnp.int32, (8, vd), 0)
    terms = jnp.where(kind == 0, vx, jnp.where(kind == 1, vy, vz)) * -2.0
    terms = jnp.where(kind < 3, terms, jnp.where(kind == 3, vx * vx + vy * vy + vz * vz, 1.0)) * (wavenum * wavenum)
    terms = jnp.where(kind < 6, terms, 0.0)
    parts = []
    for _ in range(3):
        parts.append(terms.astype(BF16).astype(F32))
        terms = terms - parts[-1]
    right = jnp.concatenate(parts + [jnp.zeros((LANES - 24, vd), F32)], axis=0).astype(BF16)
    kind = lax.broadcasted_iota(jnp.int32, (8, LANES), 0)
    for base in range(0, chans, LANES):
        points = elem_ref[:, base:base + LANES]
        ex, ey, ez = points[0:1], points[1:2], points[2:3]
        norm = ex * ex + ey * ey + ez * ez
        low = jnp.bitwise_and(norm, 15)
        facts = jnp.where(kind == 0, ex, jnp.where(kind == 1, ey, jnp.where(kind == 2, ez, 1)))
        facts = jnp.where(kind < 4, facts, jnp.where(kind == 4, norm - low, jnp.where(kind == 5, low, 0))).astype(F32)
        facts = jnp.concatenate([facts, facts, facts, jnp.zeros((LANES - 24, LANES), F32)], axis=0)
        elem[base:base + LANES, :] = facts.T.astype(BF16)
        heights[base:base + LANES, :] = jnp.broadcast_to(ez.astype(F32) * wavenum, (LANES, LANES)).T
    squares[...] = dot(elem[...], right)

    tall = cl // TALL
    steps = nc * tall

    def make_operator(low, high):
        @pl.loop(low, high)
        def _(step):
            block = lax.rem(me_c + lax.div(step, tall), nc)
            place = pl.ds(pl.multiple_of(block * cl + lax.rem(step, tall) * TALL, TALL), TALL)
            ez = heights[place, :]
            for base in range(0, vd, LANES):
                lanes = slice(base, base + LANES)
                vz, square = vox[:, lanes], squares[place, lanes]
                inv = lax.rsqrt(square)
                turns = vz + square * inv
                turns = turns - ((turns + ROUND) - ROUND)
                sine = turns * horner(sin_poly, turns * turns)
                rest = scale - sine * sine
                cosine = rest * lax.rsqrt(rest)
                twice = (vz - ez) * inv
                oper[0, place, lanes] = (twice * (rest - 0.5 * scale)).astype(BF16)
                oper[1, place, lanes] = (twice * sine * cosine).astype(BF16)

    def multiply(block, first=False, last=False, part_of=None):
        place = pl.ds(pl.multiple_of(block * cl, cl), cl)
        right = jnp.concatenate([oper[0, place, :], oper[1, place, :]], axis=0)
        if part_of is None:
            real, imag = rfbuf[block, 0], rfbuf[block, 1]
            wheres = (slice(0, 2 * frames),)
        else:
            some = pl.ds(pl.multiple_of(part_of * rows, rows), rows)
            real, imag = rfbuf[block, 0, some, :], rfbuf[block, 1, some, :]
            wheres = (some, pl.ds(pl.multiple_of(frames + part_of * rows, rows), rows))
        left = jnp.concatenate(
            [jnp.concatenate([real, imag], axis=1), jnp.concatenate([imag, -real], axis=1)], axis=0)
        value = dot(left, right)
        for index, where in enumerate(wheres):
            some = value if part_of is None else value[index * rows:(index + 1) * rows]
            if not first:
                some = some + acc[where, :]
            if last:
                vols[where, :] = some.astype(BF16)
            else:
                acc[where, :] = some

    width = vd // (nf // 2)

    def multiply_step(block, step):
        place = pl.ds(pl.multiple_of(block * cl, cl), cl)
        lanes = pl.ds(pl.multiple_of(step * width, width), width)
        real, imag = rfbuf[block, 0], rfbuf[block, 1]
        left = jnp.concatenate(
            [jnp.concatenate([real, imag], axis=1), jnp.concatenate([imag, -real], axis=1)], axis=0)
        acc[:, lanes] = acc[:, lanes] + dot(left, jnp.concatenate([oper[0, place, lanes], oper[1, place, lanes]], axis=0))

    pairs = stagger and nc == 4
    inside = jnp.logical_and(second, jnp.logical_and(me_c > 0, me_c < nc - 1))

    def passed_on(block):
        right = jnp.logical_and(me_c - block >= reach, me_c < nc - 1)
        return jnp.logical_or(right, jnp.logical_and(block - me_c >= reach, me_c > 0))

    begin = steps // 8
    portion = steps * 1 // 32
    rest = begin + portion * (nf - 1)
    later = rest + (steps - rest) * 8 // 8

    def let_go():
        pl.semaphore_signal(go_sem, inc=1, device_id=(me_c, me_f + 1), device_id_type=MESH)

    def run_second():
        make_operator(0, steps)

        @pl.loop(1, nf)
        def _(k):
            plane_arrival(partner(k)).wait_recv()

        own.wait()
        multiply(me_c, first=True)
        pl.semaphore_wait(go_sem, 1)

        @pl.loop(0, nf)
        def _(k):
            j = partner(k)
            for offset in (1, -1):
                pl.when(there(offset))(own_copy(j, offset).start)

    def run_first():
        make_operator(0, begin)

        @pl.loop(1, nf)
        def _(k):
            j = partner(k)
            plane_arrival(j).wait_recv()
            send_far(j)
            if portion:
                make_operator(begin + (k - 1) * portion, begin + k * portion)

        send_near(me_f, True)

        @pl.loop(1, nf)
        def _(k):
            send_near(partner(k))

        own.wait()

    if stagger:
        pl.when(second)(run_second)
    if_first(run_first)

    @pl.loop(reach, nc - 1)
    def _(hop):
        block = jnp.where(me_c >= hop, me_c - hop, me_c + hop)
        other = jnp.where(me_c >= hop, me_c + hop, nc)

        @pl.loop(0, nf)
        def _(k):
            j = partner(k)
            for which in (block, other):
                @pl.when(jnp.logical_and(which < nc, passed_on(which)))
                def _():
                    relay_copy(which, j).wait_recv()
                    relay_copy(which, j).start()

            def early():
                make_operator(rest + lax.div((later - rest) * k, nf), rest + lax.div((later - rest) * (k + 1), nf))

            if_first(early, hop == REACH)
            if pairs:
                @pl.when(jnp.logical_and(inside, hop == 2))
                def _():
                    upper = lax.div(2 * k, nf)
                    multiply_step(me_c - 1 + 2 * upper, k - upper * (nf // 2))
            if stagger:
                if_first(let_go, hop == REACH, k == GO_AT * nf // 8)

    if nc <= REACH + 1:
        if_first(lambda: make_operator(rest, later))
        if stagger:
            if_first(let_go)
    if_first(lambda: make_operator(later, steps))
    if_first(lambda: multiply(me_c, first=True))

    lower = 2 * me_c < nc
    depth = jnp.where(lower, me_c, nc - 1 - me_c)

    def block_in_turn(turn):
        place = jnp.where(turn <= depth, depth - turn, nc + depth - turn)
        place = jnp.where(depth == 0, turn, place)
        return jnp.where(lower, place, nc - 1 - place)

    def arrive(block, low=0, high=nf):
        @pl.when(jnp.logical_not(passed_on(block)))
        def _():
            @pl.loop(low, high)
            def _(k):
                j = partner(k)
                line_copy(block, j, block, relay_send.at[block * nf + j]).wait_recv()

    @pl.loop(1, jnp.where(inside, 1, nc - 1) if pairs else nc - 1)
    def _(turn):
        block = block_in_turn(turn)
        arrive(block)
        multiply(block)

    block = block_in_turn(jnp.where(inside, 2, nc - 1) if pairs else nc - 1)
    near = lax.div(me_f, nf // 2)
    arrive(block, 0, nf // 2)
    multiply(block, last=True, part_of=near)
    arrive(block, nf // 2, nf)
    multiply(block, last=True, part_of=1 - near)

    real, imag = vols[:frames, :], vols[frames:, :]
    both = jnp.concatenate([real, imag], axis=1)
    gram_re = dot_nt(both, both)
    gram_im = dot_nt(jnp.concatenate([real, -imag], axis=1), jnp.concatenate([imag, real], axis=1))
    across = lax.broadcasted_iota(jnp.int32, (frames, frames), 1)
    down = lax.broadcasted_iota(jnp.int32, (frames, frames), 0)
    part[...] = jnp.where(down <= across, gram_re, gram_im).astype(BF16)

    members = [(c, t) for c in range(nc) for t in range(share)]

    def device(member):
        return member[0], me_bin * share + member[1]

    def is_me(member):
        return jnp.logical_and(me_c == member[0], me_sub == member[1])

    def half(index):
        return pl.ds(index * rows, rows)

    def scatter(index, source=None):
        origin = me_c * share + me_sub if source is None else members.index(source)
        return pltpu.make_async_remote_copy(
            src_ref=part.at[half(index)], dst_ref=slabs.at[origin],
            send_sem=rs_send.at[index], recv_sem=rs_recv.at[origin],
            device_id=device(owners[index]), device_id_type=MESH)

    def gather(index, member):
        place = total.at[half(index)]
        return pltpu.make_async_remote_copy(
            src_ref=place, dst_ref=place, send_sem=ag_send.at[members.index(member)], recv_sem=ag_recv.at[index],
            device_id=device(member), device_id_type=MESH)

    upper_half = 2 * me_c >= nc
    for turn in range(2):
        for index in range(2):
            across_line = upper_half if index == 0 else jnp.logical_not(upper_half)
            chosen = across_line if turn == 0 else jnp.logical_not(across_line)

            @pl.when(jnp.logical_and(chosen, jnp.logical_not(is_me(owners[index]))))
            def _():
                scatter(index).start()
    for index in range(2):
        @pl.when(is_me(owners[index]))
        def _():
            others = sorted(
                (m for m in members if m != owners[index]), key=lambda m: abs(m[0] - owners[index][0]))
            summed = part[half(index), :].astype(F32)
            for member in others:
                scatter(index, member).wait_recv()
                summed = summed + slabs[members.index(member)].astype(F32)
            total[half(index), :] = summed.astype(BF16)
            for member in others[::-1]:
                gather(index, member).start()
    for index in range(2):
        @pl.when(jnp.logical_not(is_me(owners[index])))
        def _():
            gather(index, owners[index]).wait_recv()

    packed = total[...].astype(F32)
    turned = total[...].T.astype(F32)
    same = down == across
    g_re = jnp.where(down <= across, packed, turned)
    g_im = jnp.where(down > across, packed, jnp.where(same, 0.0, -turned))
    norm = packed * packed
    norm = jnp.where(same, norm, norm + norm)
    norm = jnp.sum(jnp.sum(norm, axis=0, keepdims=True), axis=1, keepdims=True)
    factor = 4.0 / jnp.sqrt(norm + EPSILON)
    first = jnp.concatenate([g_re, g_im], axis=1).astype(BF16)
    below = jnp.concatenate([-g_im, g_re], axis=1).astype(BF16)
    rhs = jnp.concatenate([first, below], axis=0)
    second_power = dot(first, rhs)
    third_power = dot(second_power.astype(BF16), rhs)
    poly = factor * (factor * (0.3 * second_power - (0.03 * factor) * third_power) - first.astype(F32))
    h_re = (jnp.where(same, 1.0, 0.0) + poly[:, :frames]).astype(BF16)
    h_im = poly[:, frames:].astype(BF16)
    hmat[:frames, :frames] = h_re
    hmat[:frames, frames:] = h_im
    hmat[frames:, :frames] = -h_im
    hmat[frames:, frames:] = h_re

    def out_copy(j, arriving=False):
        return pltpu.make_async_remote_copy(
            src_ref=sent.at[:, piece(j)], dst_ref=out_ref.at[j if arriving else me_f],
            send_sem=out_send.at[j], recv_sem=out_recv.at[j if arriving else me_f],
            device_id=(me_c, j), device_id_type=MESH)

    height = 2 * fl
    for k in range(nf - 2, -1, -2):
        near, far = partner(k), partner(k + 1)
        start = pl.multiple_of(lax.div(near, 2) * height, height)
        place = pl.ds(start, height)
        lhs = jnp.concatenate([hmat[place, :], hmat[pl.ds(frames + start, height), :]], axis=0)
        value = dot(lhs, vols[...]).astype(BF16)
        sent[0, place, :] = value[:height]
        sent[1, place, :] = value[height:]
        out_copy(far).start()
        if k:
            out_copy(near).start()
    own_out = pltpu.make_async_copy(sent.at[:, mine], out_ref.at[me_f], out_own)
    own_out.start()

    @pl.loop(1, nf)
    def _(k):
        plane_copy(partner(k)).wait_send()

    @pl.loop(0, nf)
    def _(j):
        for offset in range(1, REACH + 1):
            for signed in (offset, -offset):
                sent_it = there(signed) if offset == 1 else jnp.logical_and(there(signed), reach >= offset)

                @pl.when(sent_it)
                def _():
                    own_copy(j, signed).wait_send()

        @pl.loop(0, nc)
        def _(block):
            @pl.when(passed_on(block))
            def _():
                relay_copy(block, j).wait_send()

    for index in range(2):
        @pl.when(jnp.logical_not(is_me(owners[index])))
        def _():
            scatter(index).wait_send()

        @pl.when(is_me(owners[index]))
        def _():
            for member in members:
                if member != owners[index]:
                    gather(index, member).wait_send()
    own_out.wait()

    @pl.loop(1, nf)
    def _(k):
        j = partner(k)
        out_copy(j).wait_send()
        out_copy(j, True).wait_recv()


def shards(nc, nf, rf_data, elem_pos, vox_pos, subbands):
    nbins, fl, cl = rf_data.shape[1:]
    frames = fl * nf
    chans = cl * nc
    share = nf // nbins
    vl = vox_pos.shape[1]
    vd = vl // share
    group = nc * share
    dma = pltpu.SemaphoreType.DMA
    inputs = [pltpu.with_memory_space_constraint(x, pltpu.HBM) for x in (rf_data, elem_pos, vox_pos, subbands)]
    received = pl.pallas_call(
        functools.partial(kernel, nc, nf, nbins),
        out_shape=pltpu.VMEM((nf, 2, fl, vd), BF16),
        in_specs=[pl.BlockSpec(memory_space=pl.ANY)] * 4,
        out_specs=pl.BlockSpec(memory_space=pl.ANY),
        scratch_shapes=[
            pltpu.VMEM((nc, 2, frames, cl), BF16),
            pltpu.VMEM(elem_pos.shape, elem_pos.dtype),
            pltpu.VMEM(vox_pos.shape, vox_pos.dtype),
            pltpu.SMEM(subbands.shape, subbands.dtype),
            dma((3,)),
            pltpu.VMEM((chans, LANES), BF16),
            pltpu.VMEM((chans, LANES), F32),
            pltpu.VMEM((1, vd), F32),
            pltpu.VMEM((chans, vd), F32),
            pltpu.VMEM((2, chans, vd), BF16),
            pltpu.VMEM((2 * frames, vd), F32),
            pltpu.VMEM((2 * frames, vd), BF16),
            pltpu.VMEM((frames, frames), BF16),
            pltpu.VMEM((group, frames // 2, frames), BF16),
            pltpu.VMEM((frames, frames), BF16),
            pltpu.VMEM((2 * frames, 2 * frames), BF16),
            pltpu.VMEM((2, frames, vd), BF16),
            pltpu.SemaphoreType.REGULAR, pltpu.SemaphoreType.REGULAR, dma, dma((nf,)), dma((nf,)),
            dma((2 * REACH * nf,)), dma((nc * nf,)), dma((nc * nf,)),
            dma((2,)), dma((group,)), dma((group,)), dma((2,)),
            dma, dma((nf,)), dma((nf,)),
        ],
        compiler_params=pltpu.CompilerParams(
            collective_id=0, has_side_effects=True, vmem_limit_bytes=40 * 2**20),
    )(*inputs)
    received = received.reshape(nbins, share, 2, fl, vd)
    return jnp.transpose(received, (3, 2, 0, 1, 4)).reshape(fl, 2, nbins, vl)


def solution(mesh):
    return jax.shard_map(
        functools.partial(shards, mesh.shape["chan"], mesh.shape["frame"]),
        mesh=mesh,
        in_specs=(P(None, None, "frame", "chan"), P(), P(None, "chan"), P()),
        out_specs=P("frame", None, None, "chan"),
        check_vma=False,
    )
```

```python
import functools
import math

import jax
import jax.numpy as jnp
from jax import lax
from jax.experimental import pallas as pl
from jax.experimental.pallas import tpu as pltpu
from jax.sharding import PartitionSpec as P

EPSILON = 1e-06
MESH = pl.DeviceIdType.MESH
F32 = jnp.float32
BF16 = jnp.bfloat16
SIN_POLY = (3.1415820121765137, -5.167142868041992, 2.5418989658355713, -0.5546361804008484)
BELOW_ONE = 1.0 - 2e-6
LANES = 128
ROUND = 12582912.0
TALL = 64
REACH = 2
GO_AT = 7
SECOND_REACH = 1


def horner(coefs, z):
    value = coefs[-1] * z + coefs[-2]
    for coef in coefs[-3::-1]:
        value = value * z + coef
    return value


def dot(a, b):
    return jnp.dot(a, b, preferred_element_type=F32)


def dot_nt(a, b):
    return lax.dot_general(a, b, (((1,), (1,)), ((), ())), preferred_element_type=F32)


def kernel(
    nc, nf, nbins,
    rf_ref, elem_hbm, vox_hbm, sub_hbm, out_ref,
    rfbuf, elem_ref, vox_ref, sub_ref, in_sem, elem, heights, vox, squares, oper, acc, vols, part, slabs, total, hmat, sent,
    met_sem, go_sem, own_sem, plane_send, plane_recv, line_send, relay_send, line_recv,
    rs_send, rs_recv, ag_send, ag_recv, out_own, out_send, out_recv,
):
    share = nf // nbins
    stagger = share == 1 and nf % 2 == 0
    frames = rfbuf.shape[2]
    cl = rfbuf.shape[3]
    chans = nc * cl
    vd = vols.shape[1]
    fl = frames // nf
    rows = frames // 2
    owners = ((nc // 2 - 1, 0), (nc // 2, 0))
    me_c = lax.axis_index("chan")
    me_f = lax.axis_index("frame")
    me_bin = lax.div(me_f, share)
    me_sub = lax.rem(me_f, share)
    second = lax.rem(me_f, 2) == 1
    first_core = jnp.logical_not(second)
    def partner(k):
        j = 0
        bit = 1
        while bit < nf:
            a = lax.rem(lax.div(me_f, bit), 2)
            b = k // bit % 2 if isinstance(k, int) else lax.rem(lax.div(k, bit), 2)
            j = j + bit * (a + b - 2 * a * b)
            bit *= 2
        return j

    reach = jnp.where(second, SECOND_REACH, REACH) if stagger else REACH

    def if_first(run, *conditions):
        for condition in conditions + ((first_core,) if stagger else ()):
            run = functools.partial(pl.when(condition), run)
        run()

    def piece(j):
        return pl.ds(pl.multiple_of(j * fl, fl), fl)

    base_f = me_f - lax.rem(me_f, 2)
    barrier = pltpu.get_barrier_semaphore()
    for step in range(2, nf, 2):
        pl.semaphore_signal(barrier, inc=1, device_id=(me_c, lax.rem(base_f + step, nf)), device_id_type=MESH)

    @pl.when(second)
    def _():
        pl.semaphore_signal(barrier, inc=1, device_id=(me_c, base_f), device_id_type=MESH)

    for step in range(1, nc):
        pl.semaphore_signal(barrier, inc=1, device_id=(lax.rem(me_c + step, nc), base_f + 1), device_id_type=MESH)

    mine = piece(me_f)
    loads = [
        pltpu.make_async_copy(source, place, in_sem.at[index])
        for index, (source, place) in enumerate(
            ((elem_hbm, elem_ref), (vox_hbm, vox_ref), (sub_hbm, sub_ref)))
    ]
    for load in loads:
        load.start()
    own = pltpu.make_async_copy(rf_ref.at[:, me_bin], rfbuf.at[me_c, :, mine], own_sem)
    own.start()

    @pl.when(first_core)
    def _():
        pl.semaphore_wait(barrier, nf - 1)
        pl.semaphore_signal(met_sem, inc=1, device_id=(me_c, base_f + 1), device_id_type=MESH)

    @pl.when(second)
    def _():
        pl.semaphore_wait(met_sem, 1)

    def plane_copy(j):
        return pltpu.make_async_remote_copy(
            src_ref=rf_ref.at[:, lax.div(j, share)], dst_ref=rfbuf.at[me_c, :, mine],
            send_sem=plane_send.at[j], recv_sem=plane_recv.at[me_f],
            device_id=(me_c, j), device_id_type=MESH)

    def plane_arrival(j):
        return pltpu.make_async_remote_copy(
            src_ref=rf_ref.at[:, 0], dst_ref=rfbuf.at[me_c, :, piece(j)], send_sem=plane_send.at[j],
            recv_sem=plane_recv.at[j], device_id=(me_c, j), device_id_type=MESH)

    def line_copy(block, j, target, send_sem, mine_too=False):
        place = rfbuf.at[block, :, piece(j)]
        return pltpu.make_async_remote_copy(
            src_ref=rf_ref.at[:, me_bin] if mine_too else place, dst_ref=place,
            send_sem=send_sem, recv_sem=line_recv.at[block * nf + j],
            device_id=(target, me_f), device_id_type=MESH)

    def own_copy(j, offset, mine_too=False):
        slot = offset + REACH - (offset > 0)
        return line_copy(me_c, j, me_c + offset, line_send.at[slot * nf + j], mine_too)

    def relay_copy(block, j):
        target = jnp.where(block < me_c, me_c + 1, me_c - 1)
        return line_copy(block, j, target, relay_send.at[block * nf + j])

    def there(offset):
        return me_c + offset < nc if offset > 0 else me_c + offset >= 0

    def send_far(j, mine_too=False):
        for offset in range(REACH, 0, -1):
            for signed in (offset, -offset):
                farther = signed + (1 if signed > 0 else -1)
                condition = there(signed)
                if offset < REACH:
                    condition = jnp.logical_and(condition, jnp.logical_not(there(farther)))

                @pl.when(condition)
                def _():
                    own_copy(j, signed, mine_too).start()

    def send_near(j, mine_too=False):
        for offset in range(REACH - 1, 0, -1):
            for signed in (offset, -offset):
                @pl.when(there(signed + (1 if signed > 0 else -1)))
                def _():
                    own_copy(j, signed, mine_too).start()

    for parity in (0, 1):
        for k in range(0, nf, 2):
            j = lax.rem(base_f + k, nf) + parity
            if k == 0:
                @pl.when(j != me_f)
                def _():
                    plane_copy(j).start()
            else:
                plane_copy(j).start()

    @pl.when(first_core)
    def _():
        pl.semaphore_wait(met_sem, 1)

    @pl.when(second)
    def _():
        pl.semaphore_wait(barrier, (nc - 1) * 2)
        pl.semaphore_signal(met_sem, inc=1, device_id=(me_c, base_f), device_id_type=MESH)

    if_first(lambda: send_far(me_f, True))

    def send_next(j, mine_too=False):
        for offset in (1, -1):
            pl.when(there(offset))(own_copy(j, offset, mine_too).start)

    if stagger:
        pl.when(second)(functools.partial(send_next, me_f, True))

    scale = 2.0 / math.sqrt(chans)
    sin_poly = [coef * math.sqrt(scale) * BELOW_ONE for coef in SIN_POLY]
    for load in loads:
        load.wait()
    wavenum = (32.0 + sub_ref[me_bin].astype(F32)) / 64.0
    voxels = vox_ref[:, pl.ds(pl.multiple_of(me_sub * vd, LANES), vd)].astype(F32)
    vx, vy, vz = voxels[0:1], voxels[1:2], voxels[2:3]
    vox[...] = vz * wavenum
    kind = lax.broadcasted_iota(jnp.int32, (8, vd), 0)
    terms = jnp.where(kind == 0, vx, jnp.where(kind == 1, vy, vz)) * -2.0
    terms = jnp.where(kind < 3, terms, jnp.where(kind == 3, vx * vx + vy * vy + vz * vz, 1.0)) * (wavenum * wavenum)
    terms = jnp.where(kind < 6, terms, 0.0)
    parts = []
    for _ in range(3):
        parts.append(terms.astype(BF16).astype(F32))
        terms = terms - parts[-1]
    right = jnp.concatenate(parts + [jnp.zeros((LANES - 24, vd), F32)], axis=0).astype(BF16)
    kind = lax.broadcasted_iota(jnp.int32, (8, LANES), 0)
    for base in range(0, chans, LANES):
        points = elem_ref[:, base:base + LANES]
        ex, ey, ez = points[0:1], points[1:2], points[2:3]
        norm = ex * ex + ey * ey + ez * ez
        low = jnp.bitwise_and(norm, 15)
        facts = jnp.where(kind == 0, ex, jnp.where(kind == 1, ey, jnp.where(kind == 2, ez, 1)))
        facts = jnp.where(kind < 4, facts, jnp.where(kind == 4, norm - low, jnp.where(kind == 5, low, 0))).astype(F32)
        facts = jnp.concatenate([facts, facts, facts, jnp.zeros((LANES - 24, LANES), F32)], axis=0)
        elem[base:base + LANES, :] = facts.T.astype(BF16)
        heights[base:base + LANES, :] = jnp.broadcast_to(ez.astype(F32) * wavenum, (LANES, LANES)).T
    squares[...] = dot(elem[...], right)

    tall = cl // TALL
    steps = nc * tall

    def make_operator(low, high):
        @pl.loop(low, high)
        def _(step):
            block = lax.rem(me_c + lax.div(step, tall), nc)
            place = pl.ds(pl.multiple_of(block * cl + lax.rem(step, tall) * TALL, TALL), TALL)
            ez = heights[place, :]
            for base in range(0, vd, LANES):
                lanes = slice(base, base + LANES)
                vz, square = vox[:, lanes], squares[place, lanes]
                inv = lax.rsqrt(square)
                turns = vz + square * inv
                turns = turns - ((turns + ROUND) - ROUND)
                sine = turns * horner(sin_poly, turns * turns)
                rest = scale - sine * sine
                cosine = rest * lax.rsqrt(rest)
                twice = (vz - ez) * inv
                oper[0, place, lanes] = (twice * (rest - 0.5 * scale)).astype(BF16)
                oper[1, place, lanes] = (twice * sine * cosine).astype(BF16)

    def multiply(block, first=False, last=False, part_of=None):
        place = pl.ds(pl.multiple_of(block * cl, cl), cl)
        right = jnp.concatenate([oper[0, place, :], oper[1, place, :]], axis=0)
        if part_of is None:
            real, imag = rfbuf[block, 0], rfbuf[block, 1]
            wheres = (slice(0, 2 * frames),)
        else:
            some = pl.ds(pl.multiple_of(part_of * rows, rows), rows)
            real, imag = rfbuf[block, 0, some, :], rfbuf[block, 1, some, :]
            wheres = (some, pl.ds(pl.multiple_of(frames + part_of * rows, rows), rows))
        left = jnp.concatenate(
            [jnp.concatenate([real, imag], axis=1), jnp.concatenate([imag, -real], axis=1)], axis=0)
        value = dot(left, right)
        for index, where in enumerate(wheres):
            some = value if part_of is None else value[index * rows:(index + 1) * rows]
            if not first:
                some = some + acc[where, :]
            if last:
                vols[where, :] = some.astype(BF16)
            else:
                acc[where, :] = some

    width = vd // (nf // 2)

    def multiply_step(block, step):
        place = pl.ds(pl.multiple_of(block * cl, cl), cl)
        lanes = pl.ds(pl.multiple_of(step * width, width), width)
        real, imag = rfbuf[block, 0], rfbuf[block, 1]
        left = jnp.concatenate(
            [jnp.concatenate([real, imag], axis=1), jnp.concatenate([imag, -real], axis=1)], axis=0)
        acc[:, lanes] = acc[:, lanes] + dot(left, jnp.concatenate([oper[0, place, lanes], oper[1, place, lanes]], axis=0))

    pairs = stagger and nc == 4
    inside = jnp.logical_and(second, jnp.logical_and(me_c > 0, me_c < nc - 1))

    def passed_on(block):
        right = jnp.logical_and(me_c - block >= reach, me_c < nc - 1)
        return jnp.logical_or(right, jnp.logical_and(block - me_c >= reach, me_c > 0))

    begin = steps // 8
    portion = 0
    rest = begin + portion * (nf - 1)
    later = rest + (steps - rest) * 8 // 8

    def let_go():
        pl.semaphore_signal(go_sem, inc=1, device_id=(me_c, me_f + 1), device_id_type=MESH)

    def run_second():
        make_operator(0, steps // 8)
        plane_arrival(partner(1)).wait_recv()
        send_next(partner(1))
        make_operator(steps // 8, steps)

        @pl.loop(2, nf)
        def _(k):
            plane_arrival(partner(k)).wait_recv()

        own.wait()
        multiply(me_c, first=True)
        pl.semaphore_wait(go_sem, 1)

        @pl.loop(2, nf)
        def _(k):
            send_next(partner(k))

    def run_first():
        make_operator(0, begin)

        @pl.loop(1, nf)
        def _(k):
            j = partner(k)
            plane_arrival(j).wait_recv()
            send_far(j)
            if portion:
                make_operator(begin + (k - 1) * portion, begin + k * portion)

        send_near(me_f, True)

        @pl.loop(1, nf)
        def _(k):
            send_near(partner(k))

        own.wait()

    if stagger:
        pl.when(second)(run_second)
    if_first(run_first)

    @pl.loop(jnp.where(inside, nc - 1, reach) if pairs else reach, nc - 1)
    def _(hop):
        block = jnp.where(me_c >= hop, me_c - hop, me_c + hop)
        other = jnp.where(me_c >= hop, me_c + hop, nc)

        @pl.loop(0, nf)
        def _(k):
            j = partner(k)
            for which in (block, other):
                @pl.when(jnp.logical_and(which < nc, passed_on(which)))
                def _():
                    relay_copy(which, j).wait_recv()
                    relay_copy(which, j).start()

            def early():
                make_operator(rest + lax.div((later - rest) * k, nf), rest + lax.div((later - rest) * (k + 1), nf))

            if_first(early, hop == REACH)
            if stagger:
                if_first(let_go, hop == REACH, k == GO_AT * nf // 8)

    def pass_all_on():
        low_side = 2 * me_c < nc
        outer = jnp.where(low_side, me_c - 1, me_c + 1)
        inner = jnp.where(low_side, me_c + 1, me_c - 1)
        before = None
        for block in (outer, inner, jnp.where(low_side, nc - 1, 0)):
            @pl.loop(0, nf)
            def _(k):
                j = partner(k)
                relay_copy(block, j).wait_recv()
                relay_copy(block, j).start()
                if before is not None:
                    pl.when(k < nf // 2)(functools.partial(multiply_step, before, k))

            before = block

    if pairs:
        pl.when(inside)(pass_all_on)

    if nc <= REACH + 1:
        if_first(lambda: make_operator(rest, later))
        if stagger:
            if_first(let_go)
    if_first(lambda: make_operator(later, steps))
    if_first(lambda: multiply(me_c, first=True))

    lower = 2 * me_c < nc
    depth = jnp.where(lower, me_c, nc - 1 - me_c)

    def block_in_turn(turn):
        place = jnp.where(turn <= depth, depth - turn, nc + depth - turn)
        place = jnp.where(depth == 0, turn, place)
        return jnp.where(lower, place, nc - 1 - place)

    def arrive(block, low=0, high=nf):
        @pl.when(jnp.logical_not(passed_on(block)))
        def _():
            @pl.loop(low, high)
            def _(k):
                j = partner(k)
                line_copy(block, j, block, relay_send.at[block * nf + j]).wait_recv()

    @pl.loop(1, jnp.where(inside, 1, nc - 1) if pairs else nc - 1)
    def _(turn):
        block = block_in_turn(turn)
        arrive(block)
        multiply(block)

    block = block_in_turn(jnp.where(inside, 2, nc - 1) if pairs else nc - 1)
    near = lax.div(me_f, nf // 2)
    arrive(block, 0, nf // 2)
    multiply(block, last=True, part_of=near)
    arrive(block, nf // 2, nf)
    multiply(block, last=True, part_of=1 - near)

    real, imag = vols[:frames, :], vols[frames:, :]
    both = jnp.concatenate([real, imag], axis=1)
    gram_re = dot_nt(both, both)
    gram_im = dot_nt(jnp.concatenate([real, -imag], axis=1), jnp.concatenate([imag, real], axis=1))
    across = lax.broadcasted_iota(jnp.int32, (frames, frames), 1)
    down = lax.broadcasted_iota(jnp.int32, (frames, frames), 0)
    part[...] = jnp.where(down <= across, gram_re, gram_im).astype(BF16)

    members = [(c, t) for c in range(nc) for t in range(share)]

    def device(member):
        return member[0], me_bin * share + member[1]

    def is_me(member):
        return jnp.logical_and(me_c == member[0], me_sub == member[1])

    def half(index):
        return pl.ds(index * rows, rows)

    def scatter(index, source=None):
        origin = me_c * share + me_sub if source is None else members.index(source)
        return pltpu.make_async_remote_copy(
            src_ref=part.at[half(index)], dst_ref=slabs.at[origin],
            send_sem=rs_send.at[index], recv_sem=rs_recv.at[origin],
            device_id=device(owners[index]), device_id_type=MESH)

    def gather(index, member):
        place = total.at[half(index)]
        return pltpu.make_async_remote_copy(
            src_ref=place, dst_ref=place, send_sem=ag_send.at[members.index(member)], recv_sem=ag_recv.at[index],
            device_id=device(member), device_id_type=MESH)

    upper_half = 2 * me_c >= nc
    for turn in range(2):
        for index in range(2):
            across_line = upper_half if index == 0 else jnp.logical_not(upper_half)
            chosen = across_line if turn == 0 else jnp.logical_not(across_line)

            @pl.when(jnp.logical_and(chosen, jnp.logical_not(is_me(owners[index]))))
            def _():
                scatter(index).start()
    for index in range(2):
        @pl.when(is_me(owners[index]))
        def _():
            others = sorted(
                (m for m in members if m != owners[index]), key=lambda m: abs(m[0] - owners[index][0]))
            summed = part[half(index), :].astype(F32)
            for member in others:
                scatter(index, member).wait_recv()
                summed = summed + slabs[members.index(member)].astype(F32)
            total[half(index), :] = summed.astype(BF16)
            for member in others[::-1]:
                gather(index, member).start()
    for index in range(2):
        @pl.when(jnp.logical_not(is_me(owners[index])))
        def _():
            gather(index, owners[index]).wait_recv()

    packed = total[...].astype(F32)
    turned = total[...].T.astype(F32)
    same = down == across
    g_re = jnp.where(down <= across, packed, turned)
    g_im = jnp.where(down > across, packed, jnp.where(same, 0.0, -turned))
    norm = packed * packed
    norm = jnp.where(same, norm, norm + norm)
    norm = jnp.sum(jnp.sum(norm, axis=0, keepdims=True), axis=1, keepdims=True)
    factor = 4.0 / jnp.sqrt(norm + EPSILON)
    first = jnp.concatenate([g_re, g_im], axis=1).astype(BF16)
    below = jnp.concatenate([-g_im, g_re], axis=1).astype(BF16)
    rhs = jnp.concatenate([first, below], axis=0)
    second_power = dot(first, rhs)
    third_power = dot(second_power.astype(BF16), rhs)
    poly = factor * (factor * (0.3 * second_power - (0.03 * factor) * third_power) - first.astype(F32))
    h_re = (jnp.where(same, 1.0, 0.0) + poly[:, :frames]).astype(BF16)
    h_im = poly[:, frames:].astype(BF16)
    hmat[:frames, :frames] = h_re
    hmat[:frames, frames:] = h_im
    hmat[frames:, :frames] = -h_im
    hmat[frames:, frames:] = h_re

    def out_copy(j, arriving=False):
        return pltpu.make_async_remote_copy(
            src_ref=sent.at[:, piece(j)], dst_ref=out_ref.at[j if arriving else me_f],
            send_sem=out_send.at[j], recv_sem=out_recv.at[j if arriving else me_f],
            device_id=(me_c, j), device_id_type=MESH)

    height = 2 * fl
    for k in range(nf - 2, -1, -2):
        near, far = partner(k), partner(k + 1)
        start = pl.multiple_of(lax.div(near, 2) * height, height)
        place = pl.ds(start, height)
        lhs = jnp.concatenate([hmat[place, :], hmat[pl.ds(frames + start, height), :]], axis=0)
        value = dot(lhs, vols[...]).astype(BF16)
        sent[0, place, :] = value[:height]
        sent[1, place, :] = value[height:]
        out_copy(far).start()
        if k:
            out_copy(near).start()
    own_out = pltpu.make_async_copy(sent.at[:, mine], out_ref.at[me_f], out_own)
    own_out.start()

    @pl.loop(1, nf)
    def _(k):
        plane_copy(partner(k)).wait_send()

    @pl.loop(0, nf)
    def _(j):
        for offset in range(1, REACH + 1):
            for signed in (offset, -offset):
                sent_it = there(signed) if offset == 1 else jnp.logical_and(there(signed), reach >= offset)

                @pl.when(sent_it)
                def _():
                    own_copy(j, signed).wait_send()

        @pl.loop(0, nc)
        def _(block):
            @pl.when(passed_on(block))
            def _():
                relay_copy(block, j).wait_send()

    for index in range(2):
        @pl.when(jnp.logical_not(is_me(owners[index])))
        def _():
            scatter(index).wait_send()

        @pl.when(is_me(owners[index]))
        def _():
            for member in members:
                if member != owners[index]:
                    gather(index, member).wait_send()
    own_out.wait()

    @pl.loop(1, nf)
    def _(k):
        j = partner(k)
        out_copy(j).wait_send()
        out_copy(j, True).wait_recv()


def shards(nc, nf, rf_data, elem_pos, vox_pos, subbands):
    nbins, fl, cl = rf_data.shape[1:]
    frames = fl * nf
    chans = cl * nc
    share = nf // nbins
    vl = vox_pos.shape[1]
    vd = vl // share
    group = nc * share
    dma = pltpu.SemaphoreType.DMA
    inputs = [pltpu.with_memory_space_constraint(x, pltpu.HBM) for x in (rf_data, elem_pos, vox_pos, subbands)]
    received = pl.pallas_call(
        functools.partial(kernel, nc, nf, nbins),
        out_shape=pltpu.VMEM((nf, 2, fl, vd), BF16),
        in_specs=[pl.BlockSpec(memory_space=pl.ANY)] * 4,
        out_specs=pl.BlockSpec(memory_space=pl.ANY),
        scratch_shapes=[
            pltpu.VMEM((nc, 2, frames, cl), BF16),
            pltpu.VMEM(elem_pos.shape, elem_pos.dtype),
            pltpu.VMEM(vox_pos.shape, vox_pos.dtype),
            pltpu.SMEM(subbands.shape, subbands.dtype),
            dma((3,)),
            pltpu.VMEM((chans, LANES), BF16),
            pltpu.VMEM((chans, LANES), F32),
            pltpu.VMEM((1, vd), F32),
            pltpu.VMEM((chans, vd), F32),
            pltpu.VMEM((2, chans, vd), BF16),
            pltpu.VMEM((2 * frames, vd), F32),
            pltpu.VMEM((2 * frames, vd), BF16),
            pltpu.VMEM((frames, frames), BF16),
            pltpu.VMEM((group, frames // 2, frames), BF16),
            pltpu.VMEM((frames, frames), BF16),
            pltpu.VMEM((2 * frames, 2 * frames), BF16),
            pltpu.VMEM((2, frames, vd), BF16),
            pltpu.SemaphoreType.REGULAR, pltpu.SemaphoreType.REGULAR, dma, dma((nf,)), dma((nf,)),
            dma((2 * REACH * nf,)), dma((nc * nf,)), dma((nc * nf,)),
            dma((2,)), dma((group,)), dma((group,)), dma((2,)),
            dma, dma((nf,)), dma((nf,)),
        ],
        compiler_params=pltpu.CompilerParams(
            collective_id=0, has_side_effects=True, vmem_limit_bytes=40 * 2**20),
    )(*inputs)
    received = received.reshape(nbins, share, 2, fl, vd)
    return jnp.transpose(received, (3, 2, 0, 1, 4)).reshape(fl, 2, nbins, vl)


def solution(mesh):
    return jax.shard_map(
        functools.partial(shards, mesh.shape["chan"], mesh.shape["frame"]),
        mesh=mesh,
        in_specs=(P(None, None, "frame", "chan"), P(), P(None, "chan"), P()),
        out_specs=P("frame", None, None, "chan"),
        check_vma=False,
    )
```

```python
import functools
import math

import jax
import jax.numpy as jnp
from jax import lax
from jax.experimental import pallas as pl
from jax.experimental.pallas import tpu as pltpu
from jax.sharding import PartitionSpec as P

EPSILON = 1e-06
MESH = pl.DeviceIdType.MESH
F32 = jnp.float32
BF16 = jnp.bfloat16
SIN_POLY = (3.1415820121765137, -5.167142868041992, 2.5418989658355713, -0.5546361804008484)
BELOW_ONE = 1.0 - 2e-6
LANES = 128
ROUND = 12582912.0
TALL = 64
REACH = 2
GO_AT = 7
SECOND_REACH = 1


def horner(coefs, z):
    value = coefs[-1] * z + coefs[-2]
    for coef in coefs[-3::-1]:
        value = value * z + coef
    return value


def dot(a, b):
    return jnp.dot(a, b, preferred_element_type=F32)


def dot_nt(a, b):
    return lax.dot_general(a, b, (((1,), (1,)), ((), ())), preferred_element_type=F32)


def kernel(
    nc, nf, nbins,
    rf_ref, elem_hbm, vox_hbm, sub_hbm, out_ref,
    rfbuf, elem_ref, vox_ref, sub_ref, in_sem, elem, heights, vox, squares, oper, acc, vols, part, slabs, total, hmat, sent,
    met_sem, go_sem, own_sem, plane_send, plane_recv, line_send, relay_send, line_recv,
    rs_send, rs_recv, ag_send, ag_recv, out_own, out_send, out_recv,
):
    share = nf // nbins
    stagger = share == 1 and nf % 2 == 0
    frames = rfbuf.shape[2]
    cl = rfbuf.shape[3]
    chans = nc * cl
    vd = vols.shape[1]
    fl = frames // nf
    rows = frames // 2
    owners = ((nc // 2 - 1, 0), (nc // 2, 0))
    me_c = lax.axis_index("chan")
    me_f = lax.axis_index("frame")
    me_bin = lax.div(me_f, share)
    me_sub = lax.rem(me_f, share)
    second = lax.rem(me_f, 2) == 1
    first_core = jnp.logical_not(second)
    def partner(k):
        j = 0
        bit = 1
        while bit < nf:
            a = lax.rem(lax.div(me_f, bit), 2)
            b = k // bit % 2 if isinstance(k, int) else lax.rem(lax.div(k, bit), 2)
            j = j + bit * (a + b - 2 * a * b)
            bit *= 2
        return j

    reach = jnp.where(second, SECOND_REACH, REACH) if stagger else REACH

    def if_first(run, *conditions):
        for condition in conditions + ((first_core,) if stagger else ()):
            run = functools.partial(pl.when(condition), run)
        run()

    def piece(j):
        return pl.ds(pl.multiple_of(j * fl, fl), fl)

    base_f = me_f - lax.rem(me_f, 2)
    barrier = pltpu.get_barrier_semaphore()
    for step in range(2, nf, 2):
        pl.semaphore_signal(barrier, inc=1, device_id=(me_c, lax.rem(base_f + step, nf)), device_id_type=MESH)

    @pl.when(second)
    def _():
        pl.semaphore_signal(barrier, inc=1, device_id=(me_c, base_f), device_id_type=MESH)

    for step in range(1, nc):
        pl.semaphore_signal(barrier, inc=1, device_id=(lax.rem(me_c + step, nc), base_f + 1), device_id_type=MESH)

    mine = piece(me_f)
    loads = [
        pltpu.make_async_copy(source, place, in_sem.at[index])
        for index, (source, place) in enumerate(
            ((elem_hbm, elem_ref), (vox_hbm, vox_ref), (sub_hbm, sub_ref)))
    ]
    for load in loads:
        load.start()
    own = pltpu.make_async_copy(rf_ref.at[:, me_bin], rfbuf.at[me_c, :, mine], own_sem)
    own.start()

    @pl.when(first_core)
    def _():
        pl.semaphore_wait(barrier, nf - 1)
        pl.semaphore_signal(met_sem, inc=1, device_id=(me_c, base_f + 1), device_id_type=MESH)

    @pl.when(second)
    def _():
        pl.semaphore_wait(met_sem, 1)

    def plane_copy(j):
        return pltpu.make_async_remote_copy(
            src_ref=rf_ref.at[:, lax.div(j, share)], dst_ref=rfbuf.at[me_c, :, mine],
            send_sem=plane_send.at[j], recv_sem=plane_recv.at[me_f],
            device_id=(me_c, j), device_id_type=MESH)

    def plane_arrival(j):
        return pltpu.make_async_remote_copy(
            src_ref=rf_ref.at[:, 0], dst_ref=rfbuf.at[me_c, :, piece(j)], send_sem=plane_send.at[j],
            recv_sem=plane_recv.at[j], device_id=(me_c, j), device_id_type=MESH)

    def line_copy(block, j, target, send_sem, mine_too=False):
        place = rfbuf.at[block, :, piece(j)]
        return pltpu.make_async_remote_copy(
            src_ref=rf_ref.at[:, me_bin] if mine_too else place, dst_ref=place,
            send_sem=send_sem, recv_sem=line_recv.at[block * nf + j],
            device_id=(target, me_f), device_id_type=MESH)

    def own_copy(j, offset, mine_too=False):
        slot = offset + REACH - (offset > 0)
        return line_copy(me_c, j, me_c + offset, line_send.at[slot * nf + j], mine_too)

    def relay_copy(block, j):
        target = jnp.where(block < me_c, me_c + 1, me_c - 1)
        return line_copy(block, j, target, relay_send.at[block * nf + j])

    def there(offset):
        return me_c + offset < nc if offset > 0 else me_c + offset >= 0

    def send_far(j, mine_too=False):
        for offset in range(REACH, 0, -1):
            for signed in (offset, -offset):
                farther = signed + (1 if signed > 0 else -1)
                condition = there(signed)
                if offset < REACH:
                    condition = jnp.logical_and(condition, jnp.logical_not(there(farther)))

                @pl.when(condition)
                def _():
                    own_copy(j, signed, mine_too).start()

    def send_near(j, mine_too=False):
        for offset in range(REACH - 1, 0, -1):
            for signed in (offset, -offset):
                @pl.when(there(signed + (1 if signed > 0 else -1)))
                def _():
                    own_copy(j, signed, mine_too).start()

    for parity in (0, 1):
        for k in range(0, nf, 2):
            j = lax.rem(base_f + k, nf) + parity
            if k == 0:
                @pl.when(j != me_f)
                def _():
                    plane_copy(j).start()
            else:
                plane_copy(j).start()

    @pl.when(first_core)
    def _():
        pl.semaphore_wait(met_sem, 1)

    @pl.when(second)
    def _():
        pl.semaphore_wait(barrier, (nc - 1) * 2)
        pl.semaphore_signal(met_sem, inc=1, device_id=(me_c, base_f), device_id_type=MESH)

    if_first(lambda: send_far(me_f, True))

    def send_next(j, mine_too=False):
        for offset in (1, -1):
            pl.when(there(offset))(own_copy(j, offset, mine_too).start)

    if stagger:
        pl.when(second)(functools.partial(send_next, me_f, True))

    scale = 2.0 / math.sqrt(chans)
    sin_poly = [coef * math.sqrt(scale) * BELOW_ONE for coef in SIN_POLY]
    for load in loads:
        load.wait()
    wavenum = (32.0 + sub_ref[me_bin].astype(F32)) / 64.0
    voxels = vox_ref[:, pl.ds(pl.multiple_of(me_sub * vd, LANES), vd)].astype(F32)
    vx, vy, vz = voxels[0:1], voxels[1:2], voxels[2:3]
    vox[...] = vz * wavenum
    kind = lax.broadcasted_iota(jnp.int32, (8, vd), 0)
    terms = jnp.where(kind == 0, vx, jnp.where(kind == 1, vy, vz)) * -2.0
    terms = jnp.where(kind < 3, terms, jnp.where(kind == 3, vx * vx + vy * vy + vz * vz, 1.0)) * (wavenum * wavenum)
    terms = jnp.where(kind < 6, terms, 0.0)
    parts = []
    for _ in range(3):
        parts.append(terms.astype(BF16).astype(F32))
        terms = terms - parts[-1]
    right = jnp.concatenate(parts + [jnp.zeros((LANES - 24, vd), F32)], axis=0).astype(BF16)
    kind = lax.broadcasted_iota(jnp.int32, (8, LANES), 0)
    for base in range(0, chans, LANES):
        points = elem_ref[:, base:base + LANES]
        ex, ey, ez = points[0:1], points[1:2], points[2:3]
        norm = ex * ex + ey * ey + ez * ez
        low = jnp.bitwise_and(norm, 15)
        facts = jnp.where(kind == 0, ex, jnp.where(kind == 1, ey, jnp.where(kind == 2, ez, 1)))
        facts = jnp.where(kind < 4, facts, jnp.where(kind == 4, norm - low, jnp.where(kind == 5, low, 0))).astype(F32)
        facts = jnp.concatenate([facts, facts, facts, jnp.zeros((LANES - 24, LANES), F32)], axis=0)
        elem[base:base + LANES, :] = facts.T.astype(BF16)
        heights[base:base + LANES, :] = jnp.broadcast_to(ez.astype(F32) * wavenum, (LANES, LANES)).T
    squares[...] = dot(elem[...], right)

    tall = cl // TALL
    steps = nc * tall

    def make_operator(low, high):
        @pl.loop(low, high)
        def _(step):
            block = lax.rem(me_c + lax.div(step, tall), nc)
            place = pl.ds(pl.multiple_of(block * cl + lax.rem(step, tall) * TALL, TALL), TALL)
            ez = heights[place, :]
            for base in range(0, vd, LANES):
                lanes = slice(base, base + LANES)
                vz, square = vox[:, lanes], squares[place, lanes]
                inv = lax.rsqrt(square)
                turns = vz + square * inv
                turns = turns - ((turns + ROUND) - ROUND)
                sine = turns * horner(sin_poly, turns * turns)
                rest = scale - sine * sine
                cosine = rest * lax.rsqrt(rest)
                twice = (vz - ez) * inv
                oper[0, place, lanes] = (twice * (rest - 0.5 * scale)).astype(BF16)
                oper[1, place, lanes] = (twice * sine * cosine).astype(BF16)

    def multiply(block, first=False, last=False, part_of=None):
        place = pl.ds(pl.multiple_of(block * cl, cl), cl)
        right = jnp.concatenate([oper[0, place, :], oper[1, place, :]], axis=0)
        if part_of is None:
            real, imag = rfbuf[block, 0], rfbuf[block, 1]
            wheres = (slice(0, 2 * frames),)
        else:
            some = pl.ds(pl.multiple_of(part_of * rows, rows), rows)
            real, imag = rfbuf[block, 0, some, :], rfbuf[block, 1, some, :]
            wheres = (some, pl.ds(pl.multiple_of(frames + part_of * rows, rows), rows))
        left = jnp.concatenate(
            [jnp.concatenate([real, imag], axis=1), jnp.concatenate([imag, -real], axis=1)], axis=0)
        value = dot(left, right)
        for index, where in enumerate(wheres):
            some = value if part_of is None else value[index * rows:(index + 1) * rows]
            if not first:
                some = some + acc[where, :]
            if last:
                vols[where, :] = some.astype(BF16)
            else:
                acc[where, :] = some

    width = vd // (nf // 2)

    def multiply_step(block, step):
        place = pl.ds(pl.multiple_of(block * cl, cl), cl)
        lanes = pl.ds(pl.multiple_of(step * width, width), width)
        real, imag = rfbuf[block, 0], rfbuf[block, 1]
        left = jnp.concatenate(
            [jnp.concatenate([real, imag], axis=1), jnp.concatenate([imag, -real], axis=1)], axis=0)
        acc[:, lanes] = acc[:, lanes] + dot(left, jnp.concatenate([oper[0, place, lanes], oper[1, place, lanes]], axis=0))

    pairs = stagger and nc == 4
    inside = jnp.logical_and(second, jnp.logical_and(me_c > 0, me_c < nc - 1))

    def passed_on(block):
        right = jnp.logical_and(me_c - block >= reach, me_c < nc - 1)
        return jnp.logical_or(right, jnp.logical_and(block - me_c >= reach, me_c > 0))

    begin = steps // 8
    portion = 0
    rest = begin + portion * (nf - 1)
    later = rest + (steps - rest) * 8 // 8

    def let_go():
        pl.semaphore_signal(go_sem, inc=1, device_id=(me_c, me_f + 1), device_id_type=MESH)

    def run_second():
        make_operator(0, steps * 3 // 16)
        plane_arrival(partner(1)).wait_recv()
        send_next(partner(1))
        make_operator(steps * 3 // 16, steps)

        @pl.loop(2, nf)
        def _(k):
            plane_arrival(partner(k)).wait_recv()

        own.wait()
        multiply(me_c, first=True)
        pl.semaphore_wait(go_sem, 1)

        @pl.loop(2, nf)
        def _(k):
            send_next(partner(k))

    def run_first():
        make_operator(0, begin)

        @pl.loop(1, nf)
        def _(k):
            j = partner(k)
            plane_arrival(j).wait_recv()
            send_far(j)
            if portion:
                make_operator(begin + (k - 1) * portion, begin + k * portion)

        send_near(me_f, True)

        @pl.loop(1, nf)
        def _(k):
            send_near(partner(k))

        own.wait()

    if stagger:
        pl.when(second)(run_second)
    if_first(run_first)

    @pl.loop(jnp.where(inside, nc - 1, reach) if pairs else reach, nc - 1)
    def _(hop):
        block = jnp.where(me_c >= hop, me_c - hop, me_c + hop)
        other = jnp.where(me_c >= hop, me_c + hop, nc)

        @pl.loop(0, nf)
        def _(k):
            j = partner(k)
            for which in (block, other):
                @pl.when(jnp.logical_and(which < nc, passed_on(which)))
                def _():
                    relay_copy(which, j).wait_recv()
                    relay_copy(which, j).start()

            def early():
                make_operator(rest + lax.div((later - rest) * k, nf), rest + lax.div((later - rest) * (k + 1), nf))

            if_first(early, hop == REACH)
            if stagger:
                if_first(let_go, hop == REACH, k == GO_AT * nf // 8)

    def pass_all_on():
        low_side = 2 * me_c < nc
        outer = jnp.where(low_side, me_c - 1, me_c + 1)
        inner = jnp.where(low_side, me_c + 1, me_c - 1)
        before = None
        for block in (outer, inner, jnp.where(low_side, nc - 1, 0)):
            @pl.loop(0, nf)
            def _(k):
                j = partner(k)
                relay_copy(block, j).wait_recv()
                relay_copy(block, j).start()
                if before is not None:
                    pl.when(k < nf // 2)(functools.partial(multiply_step, before, k))

            before = block

    if pairs:
        pl.when(inside)(pass_all_on)

    if nc <= REACH + 1:
        if_first(lambda: make_operator(rest, later))
        if stagger:
            if_first(let_go)
    if_first(lambda: make_operator(later, steps))
    if_first(lambda: multiply(me_c, first=True))

    lower = 2 * me_c < nc
    depth = jnp.where(lower, me_c, nc - 1 - me_c)

    def block_in_turn(turn):
        place = jnp.where(turn <= depth, depth - turn, nc + depth - turn)
        place = jnp.where(depth == 0, turn, place)
        return jnp.where(lower, place, nc - 1 - place)

    def arrive(block, low=0, high=nf):
        @pl.when(jnp.logical_not(passed_on(block)))
        def _():
            @pl.loop(low, high)
            def _(k):
                j = partner(k)
                line_copy(block, j, block, relay_send.at[block * nf + j]).wait_recv()

    @pl.loop(1, jnp.where(inside, 1, nc - 1) if pairs else nc - 1)
    def _(turn):
        block = block_in_turn(turn)
        arrive(block)
        multiply(block)

    block = block_in_turn(jnp.where(inside, 2, nc - 1) if pairs else nc - 1)
    near = lax.div(me_f, nf // 2)
    arrive(block, 0, nf // 2)
    multiply(block, last=True, part_of=near)
    arrive(block, nf // 2, nf)
    multiply(block, last=True, part_of=1 - near)

    real, imag = vols[:frames, :], vols[frames:, :]
    both = jnp.concatenate([real, imag], axis=1)
    gram_re = dot_nt(both, both)
    gram_im = dot_nt(jnp.concatenate([real, -imag], axis=1), jnp.concatenate([imag, real], axis=1))
    across = lax.broadcasted_iota(jnp.int32, (frames, frames), 1)
    down = lax.broadcasted_iota(jnp.int32, (frames, frames), 0)
    part[...] = jnp.where(down <= across, gram_re, gram_im).astype(BF16)

    members = [(c, t) for c in range(nc) for t in range(share)]

    def device(member):
        return member[0], me_bin * share + member[1]

    def is_me(member):
        return jnp.logical_and(me_c == member[0], me_sub == member[1])

    def half(index):
        return pl.ds(index * rows, rows)

    def scatter(index, source=None):
        origin = me_c * share + me_sub if source is None else members.index(source)
        return pltpu.make_async_remote_copy(
            src_ref=part.at[half(index)], dst_ref=slabs.at[origin],
            send_sem=rs_send.at[index], recv_sem=rs_recv.at[origin],
            device_id=device(owners[index]), device_id_type=MESH)

    def gather(index, member):
        place = total.at[half(index)]
        return pltpu.make_async_remote_copy(
            src_ref=place, dst_ref=place, send_sem=ag_send.at[members.index(member)], recv_sem=ag_recv.at[index],
            device_id=device(member), device_id_type=MESH)

    upper_half = 2 * me_c >= nc
    for turn in range(2):
        for index in range(2):
            across_line = upper_half if index == 0 else jnp.logical_not(upper_half)
            chosen = across_line if turn == 0 else jnp.logical_not(across_line)

            @pl.when(jnp.logical_and(chosen, jnp.logical_not(is_me(owners[index]))))
            def _():
                scatter(index).start()
    for index in range(2):
        @pl.when(is_me(owners[index]))
        def _():
            others = sorted(
                (m for m in members if m != owners[index]), key=lambda m: abs(m[0] - owners[index][0]))
            summed = part[half(index), :].astype(F32)
            for member in others:
                scatter(index, member).wait_recv()
                summed = summed + slabs[members.index(member)].astype(F32)
            total[half(index), :] = summed.astype(BF16)
            for member in others[::-1]:
                gather(index, member).start()
    for index in range(2):
        @pl.when(jnp.logical_not(is_me(owners[index])))
        def _():
            gather(index, owners[index]).wait_recv()

    packed = total[...].astype(F32)
    turned = total[...].T.astype(F32)
    same = down == across
    g_re = jnp.where(down <= across, packed, turned)
    g_im = jnp.where(down > across, packed, jnp.where(same, 0.0, -turned))
    norm = packed * packed
    norm = jnp.where(same, norm, norm + norm)
    norm = jnp.sum(jnp.sum(norm, axis=0, keepdims=True), axis=1, keepdims=True)
    factor = 4.0 / jnp.sqrt(norm + EPSILON)
    first = jnp.concatenate([g_re, g_im], axis=1).astype(BF16)
    below = jnp.concatenate([-g_im, g_re], axis=1).astype(BF16)
    rhs = jnp.concatenate([first, below], axis=0)
    second_power = dot(first, rhs)
    third_power = dot(second_power.astype(BF16), rhs)
    poly = factor * (factor * (0.3 * second_power - (0.03 * factor) * third_power) - first.astype(F32))
    h_re = (jnp.where(same, 1.0, 0.0) + poly[:, :frames]).astype(BF16)
    h_im = poly[:, frames:].astype(BF16)
    hmat[:frames, :frames] = h_re
    hmat[:frames, frames:] = h_im
    hmat[frames:, :frames] = -h_im
    hmat[frames:, frames:] = h_re

    def out_copy(j, arriving=False):
        return pltpu.make_async_remote_copy(
            src_ref=sent.at[:, piece(j)], dst_ref=out_ref.at[j if arriving else me_f],
            send_sem=out_send.at[j], recv_sem=out_recv.at[j if arriving else me_f],
            device_id=(me_c, j), device_id_type=MESH)

    height = 2 * fl
    for k in range(nf - 2, -1, -2):
        near, far = partner(k), partner(k + 1)
        start = pl.multiple_of(lax.div(near, 2) * height, height)
        place = pl.ds(start, height)
        lhs = jnp.concatenate([hmat[place, :], hmat[pl.ds(frames + start, height), :]], axis=0)
        value = dot(lhs, vols[...]).astype(BF16)
        sent[0, place, :] = value[:height]
        sent[1, place, :] = value[height:]
        out_copy(far).start()
        if k:
            out_copy(near).start()
    own_out = pltpu.make_async_copy(sent.at[:, mine], out_ref.at[me_f], out_own)
    own_out.start()

    @pl.loop(1, nf)
    def _(k):
        plane_copy(partner(k)).wait_send()

    @pl.loop(0, nf)
    def _(j):
        for offset in range(1, REACH + 1):
            for signed in (offset, -offset):
                sent_it = there(signed) if offset == 1 else jnp.logical_and(there(signed), reach >= offset)

                @pl.when(sent_it)
                def _():
                    own_copy(j, signed).wait_send()

        @pl.loop(0, nc)
        def _(block):
            @pl.when(passed_on(block))
            def _():
                relay_copy(block, j).wait_send()

    for index in range(2):
        @pl.when(jnp.logical_not(is_me(owners[index])))
        def _():
            scatter(index).wait_send()

        @pl.when(is_me(owners[index]))
        def _():
            for member in members:
                if member != owners[index]:
                    gather(index, member).wait_send()
    own_out.wait()

    @pl.loop(1, nf)
    def _(k):
        j = partner(k)
        out_copy(j).wait_send()
        out_copy(j, True).wait_recv()


def shards(nc, nf, rf_data, elem_pos, vox_pos, subbands):
    nbins, fl, cl = rf_data.shape[1:]
    frames = fl * nf
    chans = cl * nc
    share = nf // nbins
    vl = vox_pos.shape[1]
    vd = vl // share
    group = nc * share
    dma = pltpu.SemaphoreType.DMA
    inputs = [pltpu.with_memory_space_constraint(x, pltpu.HBM) for x in (rf_data, elem_pos, vox_pos, subbands)]
    received = pl.pallas_call(
        functools.partial(kernel, nc, nf, nbins),
        out_shape=pltpu.VMEM((nf, 2, fl, vd), BF16),
        in_specs=[pl.BlockSpec(memory_space=pl.ANY)] * 4,
        out_specs=pl.BlockSpec(memory_space=pl.ANY),
        scratch_shapes=[
            pltpu.VMEM((nc, 2, frames, cl), BF16),
            pltpu.VMEM(elem_pos.shape, elem_pos.dtype),
            pltpu.VMEM(vox_pos.shape, vox_pos.dtype),
            pltpu.SMEM(subbands.shape, subbands.dtype),
            dma((3,)),
            pltpu.VMEM((chans, LANES), BF16),
            pltpu.VMEM((chans, LANES), F32),
            pltpu.VMEM((1, vd), F32),
            pltpu.VMEM((chans, vd), F32),
            pltpu.VMEM((2, chans, vd), BF16),
            pltpu.VMEM((2 * frames, vd), F32),
            pltpu.VMEM((2 * frames, vd), BF16),
            pltpu.VMEM((frames, frames), BF16),
            pltpu.VMEM((group, frames // 2, frames), BF16),
            pltpu.VMEM((frames, frames), BF16),
            pltpu.VMEM((2 * frames, 2 * frames), BF16),
            pltpu.VMEM((2, frames, vd), BF16),
            pltpu.SemaphoreType.REGULAR, pltpu.SemaphoreType.REGULAR, dma, dma((nf,)), dma((nf,)),
            dma((2 * REACH * nf,)), dma((nc * nf,)), dma((nc * nf,)),
            dma((2,)), dma((group,)), dma((group,)), dma((2,)),
            dma, dma((nf,)), dma((nf,)),
        ],
        compiler_params=pltpu.CompilerParams(
            collective_id=0, has_side_effects=True, vmem_limit_bytes=40 * 2**20),
    )(*inputs)
    received = received.reshape(nbins, share, 2, fl, vd)
    return jnp.transpose(received, (3, 2, 0, 1, 4)).reshape(fl, 2, nbins, vl)


def solution(mesh):
    return jax.shard_map(
        functools.partial(shards, mesh.shape["chan"], mesh.shape["frame"]),
        mesh=mesh,
        in_specs=(P(None, None, "frame", "chan"), P(), P(None, "chan"), P()),
        out_specs=P("frame", None, None, "chan"),
        check_vma=False,
    )
```
